32 devices in a mesh: groups: 2 (over x), att: 8 (over z, y), exp: 2 (over core).
Axes of the slice: x: 2, y: 2, z: 4, core: 2. Of those that a mesh axis runs over, the one named last changes fastest.
Arguments:
- query: bfloat16 [2048, 2048], P(('groups', 'att'), 'exp'), parts along dimension 0, may hold values from -9 to 9
- new_key: bfloat16 [2048, 256], P(('groups', 'att'), 'exp'), parts along dimension 0, may hold values from -6 to 6
- new_value: bfloat16 [2048, 256], P(('groups', 'att'), 'exp'), parts along dimension 0, may hold values from -6 to 6
- cache_keys: bfloat16 [2048, 64, 256], P(('groups', 'att'), None, 'exp'), parts along dimension 0, may hold values from -9 to 9
- cache_values: bfloat16 [2048, 64, 256], P(('groups', 'att'), None, 'exp'), parts along dimension 0, may hold values from -6 to 6
- lengths: int32 [2048], P(('groups', 'att')), parts along dimension 0, may hold values from 2 to 64, as said below
- out_proj: bfloat16 [2048, 2880], P('exp'), may hold values from -0.125 to 0.125
- residual: bfloat16 [2048, 2880], P(('groups', 'att', 'exp')), parts along dimension 0, may hold values from -6 to 6
- norm_gain: float32 [2880], replicated, may hold values from 0.25 to 1.75
- router: float32 [2880, 8], replicated, may hold values from -0.21875 to 0.21875
- routes: int32 [2048, 4], P(('groups', 'att', 'exp')), parts along dimension 0, may hold values from 0 to 7, all different within a row; in each aligned block of 64 rows (0 to 63, 64 to 127, ...) at most 64 rows name the same one
- w_gate: bfloat16 [8, 2880, 1440], P('att', None, 'exp'), may hold values from -0.109375 to 0.109375
- w_up: bfloat16 [8, 2880, 1440], P('att', None, 'exp'), may hold values from -0.109375 to 0.109375
- w_down: bfloat16 [8, 1440, 2880], P('att', 'exp'), may hold values from -0.15625 to 0.15625
Outputs:
- mixed: bfloat16 [2048, 2880], P(('groups', 'att', 'exp')), parts along dimension 0
The draws below stay inside these ranges and needn't reach their ends.
There are 2 independent parts, one for each index of `groups`. The reference program is written for one: setup_inputs(seed, part) draws one part's arguments, and reference() takes and returns one part's arrays. A program takes and returns all parts, laid end to end along the dimension named above; an argument that names none is the same for every part. Nothing has to cross between parts.
Inputs may be any that keep to these rules, and one draw needn't show every extreme that they name: `routes`: each row names 4 different experts. Among the 64 rows of one device (aligned blocks in order) no expert is named more than 64 times, and that count is reached in every draw. `lengths`: every eighth request, starting with the first, uses all 64 cached positions.
All inputs are finite; a program needn't handle non-finite values.
Results may differ from the reference program's by a relative error of at most 0.0065.
Values may be sent and summed in bfloat16 or wider, within the bound.
A program may use at most 128 MiB of HBM per device.

```python
import math
import jax
import jax.numpy as jnp
import numpy as np
from jax import lax

D = 2880
QH = 32
KVH = 4
HEAD = 64
HID = 1440
TOP = 4
CACHE = 64
EXPERTS = 8
ROWS = 1024
ROW_DEV = 64
CAP = 64
N_EXP = 2


def draw_query(key, part):
    shaped = (ROWS, QH * HEAD)
    values = jnp.clip(jax.random.normal(jax.random.fold_in(key, 1), shaped, jnp.float32), -4.0, 4.0)
    return values.astype(jnp.bfloat16)


def draw_cache_keys(key, part):
    shaped = (ROWS, CACHE, KVH * HEAD)
    values = jnp.clip(jax.random.normal(jax.random.fold_in(key, 2), shaped, jnp.float32), -4.0, 4.0)
    return values.astype(jnp.bfloat16)


def draw_lengths(key, part):
    filled = jax.random.randint(jax.random.fold_in(key, 3), (ROWS,), 2, CACHE + 1)
    row_index = jnp.arange(ROWS)
    return jnp.where(row_index % 8 == 0, CACHE, filled).astype(jnp.int32)


def levels(stream_key, extent, split, least, high):
    level = 1.0
    for axis_at, shards_of in split:
        draws = jax.random.uniform(jax.random.fold_in(jax.random.fold_in(stream_key, 6), axis_at), (shards_of,), jnp.float32, least / len(split), high / len(split))
        level = level * jnp.repeat(jnp.exp(draws), extent[axis_at] // shards_of).reshape((-1,) + (1,) * (len(extent) - 1 - axis_at))
    return level


def routed_block(own_key, own, number, rows, count, top, reach, slope):
    sequence = jax.random.permutation(own_key, count)
    packed, common = shares(count, rows * top, reach, slope, True), shares(count, rows * top, reach, slope, False)
    places = jnp.arange(count)

    def named(tallies, rotation):
        used = int((tallies > 0).sum())
        fixed = max(1, used // 4)
        shifted = fixed + (places - fixed + rotation * (used - fixed)) % max(1, count - fixed)
        return jnp.zeros((count,), jnp.int32).at[sequence[jnp.where(places < fixed, places, shifted)]].set(jnp.asarray(tallies, jnp.int32))

    tallies = jnp.where(number % 4 == 0, named(packed, number // 4), named(common, number - number // 4 - 1))
    mixed = jax.random.permutation(jax.random.fold_in(own, 3), count)
    donor, sink = mixed[0:count // 2 * 2:2], mixed[1:count // 2 * 2:2]
    room = jnp.minimum(tallies[donor] - 1, reach - tallies[sink]) // 2
    room = jnp.where((donor == sequence[0]) | (sink == sequence[0]) | (tallies[sink] == 0), 0, jnp.maximum(room, 0))
    shifted = jax.random.randint(jax.random.fold_in(own, 4), (count // 2,), 0, 1 << 20) % (room + 1)
    tallies = tallies.at[donor].add(-shifted).at[sink].add(shifted)
    items = jnp.searchsorted(jnp.cumsum(tallies), jnp.arange(rows * top), side="right").astype(jnp.int32)
    grid = items.reshape(top, rows).T
    grid = grid[jax.random.permutation(jax.random.fold_in(own, 1), rows)]
    rotation = jax.random.randint(jax.random.fold_in(own, 2), (rows, 1), 0, top)
    return jnp.take_along_axis(grid, (jnp.arange(top)[None, :] + rotation) % top, axis=1)


def shares(count, total, reach, lean, full):
    portions = [(1 << 20) // math.isqrt(standing ** lean) + 1 for standing in range(1, count + 1)]
    largest = reach if full else min(reach, max(-(-total // count), total * portions[0] // sum(portions)))
    least = 1 if total - largest >= count - 1 else 0
    counts, rest = [largest] + [least] * (count - 1), total - largest - least * (count - 1)
    while rest > 0:
        movable = [i for i in range(1, count) if counts[i] < largest] or [i for i in range(1, count) if counts[i] < reach]
        whole, left = sum([portions[i] for i in movable]), rest
        for i in movable:
            extra = min(reach - counts[i], max(1, left * portions[i] // whole), rest)
            counts[i] = counts[i] + extra
            rest = rest - extra
    return np.array(counts)


def noise(stream_key, dims, scale, most, pieces=(), dtype=jnp.bfloat16):
    gain = levels(stream_key, dims, pieces, -0.22, 0.18) if pieces else 1.0
    drawn = jax.random.normal(stream_key, dims, jnp.float32) * scale * gain
    return jnp.minimum(jnp.maximum(drawn, -most), most).astype(dtype)


def setup_inputs(seed: int = 0, part: int = 0) -> dict:
    keys = jax.random.split(jax.random.key(seed), 15)
    part_keys = jax.random.split(jax.random.fold_in(keys[14], part), 15)
    query = draw_query(jax.random.fold_in(jax.random.fold_in(keys[14], part), 71), part)
    new_key = noise(part_keys[1], (ROWS, KVH * HEAD), 1.0, 6.0, ((0, 8), (1, 2)))
    new_value = noise(part_keys[2], (ROWS, KVH * HEAD), 1.0, 6.0, ((0, 8), (1, 2)))
    cache_keys = draw_cache_keys(jax.random.fold_in(jax.random.fold_in(keys[14], part), 71), part)
    cache_values = noise(part_keys[4], (ROWS, CACHE, KVH * HEAD), 1.0, 6.0, ((0, 8), (2, 2)))
    lengths = draw_lengths(jax.random.fold_in(jax.random.fold_in(keys[14], part), 71), part)
    out_proj = noise(keys[6], (QH * HEAD, D), (QH * HEAD) ** -0.5, 0.125, ((0, 2),))
    residual = noise(part_keys[7], (ROWS, D), 1.0, 6.0, ((0, 16),))
    norm_gain = jnp.clip(1.0 + 0.15 * jax.random.normal(keys[8], (D,), jnp.float32), 0.25, 1.75)
    router = noise(keys[9], (D, EXPERTS), (D // 4) ** -0.5, 0.21875, (), jnp.float32)
    routes_keys = jax.random.split(jax.random.fold_in(part_keys[10], 1), ROWS // ROW_DEV)
    routes_turns = jax.random.permutation(jax.random.fold_in(part_keys[10], 3), ROWS // ROW_DEV)
    routes = jax.vmap(lambda own, number: routed_block(jax.random.fold_in(part_keys[10], 2), own, number, ROW_DEV, EXPERTS, TOP, CAP, 2))(routes_keys, routes_turns).reshape((ROWS, TOP))
    w_gate = noise(keys[11], (EXPERTS, D, HID), D ** -0.5, 0.109375, ((0, 8), (2, 2)))
    w_up = noise(keys[12], (EXPERTS, D, HID), D ** -0.5, 0.109375, ((0, 8), (2, 2)))
    w_down = noise(keys[13], (EXPERTS, HID, D), HID ** -0.5, 0.15625, ((0, 8), (1, 2)))
    return {"query": query, "new_key": new_key, "new_value": new_value, "cache_keys": cache_keys, "cache_values": cache_values, "lengths": lengths, "out_proj": out_proj, "residual": residual, "norm_gain": norm_gain, "router": router, "routes": routes, "w_gate": w_gate, "w_up": w_up, "w_down": w_down}


def attend(query, new_key, new_value, cache_keys, cache_values, lengths):
    requests = query.shape[0]
    group_size = QH // KVH
    inverse_root = 1.0 / math.sqrt(HEAD)
    queries = query.astype(jnp.float32).reshape(requests, KVH, group_size, HEAD)
    cached_k = cache_keys.astype(jnp.float32).reshape(requests, CACHE, KVH, HEAD)
    cached_v = cache_values.astype(jnp.float32).reshape(requests, CACHE, KVH, HEAD)
    fresh_k = new_key.astype(jnp.float32).reshape(requests, KVH, HEAD)
    fresh_v = new_value.astype(jnp.float32).reshape(requests, KVH, HEAD)
    cached_scores = jnp.einsum('rjgd,rljd->rjgl', queries, cached_k) * inverse_root
    fresh_scores = jnp.einsum('rjgd,rjd->rjg', queries, fresh_k) * inverse_root
    live_mask = jnp.arange(CACHE)[None, :] < lengths[:, None]
    cached_scores = jnp.where(live_mask[:, None, None, :], cached_scores, -1e+30)
    highest = jnp.maximum(lax.optimization_barrier(jnp.max(cached_scores, axis=-1)), fresh_scores)
    cached_exp = jnp.exp(cached_scores - highest[..., None])
    fresh_exp = jnp.exp(fresh_scores - highest)
    totals = lax.optimization_barrier(jnp.sum(cached_exp, axis=-1)) + fresh_exp
    cached_probs = (cached_exp / totals[..., None]).astype(jnp.bfloat16)
    fresh_probs = (fresh_exp / totals).astype(jnp.bfloat16)
    output = jnp.einsum('rjgl,rljd->rjgd', cached_probs.astype(jnp.float32), cached_v)
    output = output + fresh_probs.astype(jnp.float32)[..., None] * fresh_v[:, :, None, :]
    return output.astype(jnp.bfloat16).reshape(requests, QH * HEAD)

def reference(query, new_key, new_value, cache_keys, cache_values, lengths, out_proj, residual, norm_gain, router, routes, w_gate, w_up, w_down):
    attended = attend(query, new_key, new_value, cache_keys, cache_values, lengths)
    hidden_state = residual.astype(jnp.float32) + jnp.dot(attended, out_proj, preferred_element_type=jnp.float32)
    mean_square = lax.optimization_barrier(jnp.mean(hidden_state * hidden_state, axis=-1, keepdims=True))
    normed = (hidden_state * lax.rsqrt(mean_square + 1e-05) * norm_gain).astype(jnp.bfloat16)
    logits = jnp.dot(normed.astype(jnp.float32), router, precision=lax.Precision.HIGHEST)
    chosen_logits = jnp.take_along_axis(logits, routes, axis=1)
    squashed = jax.nn.sigmoid(chosen_logits)
    gate_weights = squashed / lax.optimization_barrier(jnp.sum(squashed, axis=1, keepdims=True))
    flat_routes = routes.reshape(-1)
    most_rows = ROWS // ROW_DEV * CAP
    span = HID // N_EXP

    def one_expert(expert, table):
        picks = jnp.nonzero(flat_routes == expert, size=most_rows, fill_value=ROWS * TOP)[0].astype(jnp.int32)
        source_rows = jnp.minimum(picks // TOP, ROWS - 1).astype(jnp.int32)
        inputs = normed[source_rows]
        gate_part = jnp.dot(inputs, w_gate[expert], preferred_element_type=jnp.float32)
        up_part = jnp.dot(inputs, w_up[expert], preferred_element_type=jnp.float32)
        activated = (jax.nn.silu(gate_part) * up_part).astype(jnp.bfloat16)
        down_matrix = w_down[expert]
        total = jnp.zeros((most_rows, D), jnp.float32)
        for half in range(N_EXP):
            piece = jnp.dot(activated[:, half * span:(half + 1) * span], down_matrix[half * span:(half + 1) * span], preferred_element_type=jnp.float32)
            piece = lax.optimization_barrier(piece.astype(jnp.bfloat16))
            total = total + piece.astype(jnp.float32)
        result = total.astype(jnp.bfloat16)
        return table.at[picks].set(result, mode='drop')
    table = lax.fori_loop(0, EXPERTS, one_expert, jnp.zeros((ROWS * TOP, D), jnp.bfloat16))
    expert_out = table.reshape(ROWS, TOP, D).astype(jnp.float32)
    combined = lax.optimization_barrier(jnp.sum(gate_weights[:, :, None] * expert_out, axis=1))
    return (hidden_state + combined).astype(jnp.bfloat16)
```

```python
import functools
import math

import jax
import jax.numpy as jnp
from jax import lax
from jax.experimental import pallas as pl
from jax.experimental.pallas import tpu as pltpu
from jax.sharding import PartitionSpec as P

HEAD = 64


def attend(query, new_key, new_value, cache_keys, cache_values, lengths):
    requests = query.shape[0]
    cache_len = cache_keys.shape[1]
    value_heads = new_key.shape[1] // HEAD
    group_size = query.shape[1] // new_key.shape[1]
    inverse_root = 1.0 / math.sqrt(HEAD)
    queries = query.reshape(requests, value_heads, group_size, HEAD)
    cached_k = cache_keys.reshape(requests, cache_len, value_heads, HEAD)
    cached_v = cache_values.reshape(requests, cache_len, value_heads, HEAD)
    fresh_k = new_key.reshape(requests, value_heads, HEAD)
    fresh_v = new_value.astype(jnp.float32).reshape(requests, value_heads, HEAD)
    cached_scores = (
        jnp.einsum("rjgd,rljd->rjgl", queries, cached_k, preferred_element_type=jnp.float32)
        * inverse_root
    )
    fresh_scores = (
        jnp.einsum("rjgd,rjd->rjg", queries, fresh_k, preferred_element_type=jnp.float32)
        * inverse_root
    )
    live_mask = jnp.arange(cache_len)[None, :] < lengths[:, None]
    cached_scores = jnp.where(live_mask[:, None, None, :], cached_scores, -1e30)
    highest = jnp.maximum(jnp.max(cached_scores, axis=-1), fresh_scores)
    cached_exp = jnp.exp(cached_scores - highest[..., None])
    fresh_exp = jnp.exp(fresh_scores - highest)
    totals = jnp.sum(cached_exp, axis=-1) + fresh_exp
    cached_probs = (cached_exp / totals[..., None]).astype(jnp.bfloat16)
    fresh_probs = (fresh_exp / totals).astype(jnp.bfloat16)
    output = jnp.einsum(
        "rjgl,rljd->rjgd", cached_probs, cached_v, preferred_element_type=jnp.float32
    )
    output = output + fresh_probs.astype(jnp.float32)[..., None] * fresh_v[:, :, None, :]
    return output.astype(jnp.bfloat16).reshape(requests, query.shape[1])


INNER = 2


def moe_kernel(
    depth,
    x_ref,
    hidden_ref,
    gate_hbm,
    up_hbm,
    down_hbm,
    out_ref,
    rows_buf,
    part_buf,
    mate_buf,
    side_buf,
    line_buf,
    gate_w,
    up_w,
    down_w,
    weight_sem,
    local_sem,
    rows_send,
    rows_recv,
    mate_send,
    mate_recv,
    side_send,
    side_recv,
    line_send,
    line_recv,
):
    me = lax.axis_index("att")
    core = lax.axis_index("exp")
    other = 1 - core
    line = me // INNER
    side = me % INNER
    width = hidden_ref.shape[1]
    experts = rows_buf.shape[0]
    tokens = x_ref.shape[0]
    padded = x_ref.shape[1]

    def chip(at_line, at_side):
        return at_line * INNER + at_side

    mate_id = {"exp": other}
    side_id = {"att": chip(line, 1 - side)}
    up_id = {"att": chip(jnp.minimum(line + 1, depth - 1), side)}
    down_id = {"att": chip(jnp.maximum(line - 1, 0), side)}
    has_up = line + 1 < depth
    has_down = line >= 1
    mesh_ids = pl.DeviceIdType.MESH

    barrier = pltpu.get_barrier_semaphore()
    pl.semaphore_signal(barrier, inc=1, device_id=mate_id, device_id_type=mesh_ids)
    pl.semaphore_signal(barrier, inc=1, device_id=side_id, device_id_type=mesh_ids)

    @pl.when(has_up)
    def _():
        pl.semaphore_signal(barrier, inc=1, device_id=up_id, device_id_type=mesh_ids)

    @pl.when(has_down)
    def _():
        pl.semaphore_signal(barrier, inc=1, device_id=down_id, device_id_type=mesh_ids)

    loads = [
        pltpu.make_async_copy(gate_hbm.at[0], gate_w, weight_sem.at[0]),
        pltpu.make_async_copy(up_hbm.at[0], up_w, weight_sem.at[1]),
        pltpu.make_async_copy(down_hbm.at[0], down_w, weight_sem.at[2]),
    ]
    own_copy = pltpu.make_async_copy(x_ref, rows_buf.at[me, core], local_sem)
    own_copy.start()
    for load in loads:
        load.start()
    own_copy.wait()
    pl.semaphore_wait(barrier, 2 + has_up.astype(jnp.int32) + has_down.astype(jnp.int32))

    def rows_copy(block, kind, target):
        return pltpu.make_async_remote_copy(
            src_ref=rows_buf.at[block, core],
            dst_ref=rows_buf.at[block, core],
            send_sem=rows_send.at[block, kind],
            recv_sem=rows_recv.at[block, core],
            device_id=target,
            device_id_type=mesh_ids,
        )

    def rows_arrived(block, lane):
        pltpu.make_async_remote_copy(
            src_ref=rows_buf.at[block, lane],
            dst_ref=rows_buf.at[block, lane],
            send_sem=rows_send.at[block, 0],
            recv_sem=rows_recv.at[block, lane],
            device_id=mate_id,
            device_id_type=mesh_ids,
        ).wait_recv()

    def mate_copy(block):
        return pltpu.make_async_remote_copy(
            src_ref=part_buf.at[block, other],
            dst_ref=mate_buf.at[block],
            send_sem=mate_send.at[block],
            recv_sem=mate_recv.at[block],
            device_id=mate_id,
            device_id_type=mesh_ids,
        )

    def side_copy(at_line):
        return pltpu.make_async_remote_copy(
            src_ref=part_buf.at[chip(at_line, 1 - side), core],
            dst_ref=side_buf.at[at_line],
            send_sem=side_send.at[at_line],
            recv_sem=side_recv.at[at_line],
            device_id=side_id,
            device_id_type=mesh_ids,
        )

    def line_copy(at_line, way, target):
        return pltpu.make_async_remote_copy(
            src_ref=part_buf.at[chip(at_line, side), core],
            dst_ref=line_buf.at[way, at_line],
            send_sem=line_send.at[at_line],
            recv_sem=line_recv.at[way, at_line],
            device_id=target,
            device_id_type=mesh_ids,
        )

    def place(step, way):
        at_line = jnp.where(way == 0, line - step, line + step)
        exists = (at_line >= 0) & (at_line < depth) & ((step > 0) | (way == 0))
        exists = exists & (step >= 0) & (step < depth)
        return jnp.clip(at_line, 0, depth - 1), exists

    def expert(block):
        rows = rows_buf[block].reshape(2 * tokens, padded)
        values = rows[:, :width]
        first = (width // 128) * 128
        tail = rows[:, first:].astype(jnp.float32)
        lanes = lax.broadcasted_iota(jnp.int32, tail.shape, 1) + first - width
        chosen = (lanes == me) | (lanes == me + experts)
        weight = jnp.sum(jnp.where(chosen, tail, 0.0), axis=1, keepdims=True)
        gate = jnp.dot(values, gate_w[...], preferred_element_type=jnp.float32)
        up = jnp.dot(values, up_w[...], preferred_element_type=jnp.float32)
        activated = (gate / (1.0 + jnp.exp(-gate)) * up).astype(jnp.bfloat16)
        result = jnp.dot(activated, down_w[...], preferred_element_type=jnp.float32)
        result = (result * weight).astype(jnp.bfloat16)
        part_buf[block] = result.reshape(2, tokens, width)
        mate_copy(block).start()

    def gather_step(step, carry):
        def relay_line(way, inner):
            at_line, exists = place(step, way)
            block = chip(at_line, side)

            @pl.when(exists)
            def _():
                @pl.when(step > 0)
                def _():
                    rows_arrived(block, core)

                @pl.when(has_up & (at_line <= line))
                def _():
                    rows_copy(block, 2, up_id).start()

                @pl.when(has_down & (at_line >= line))
                def _():
                    rows_copy(block, 3, down_id).start()

                rows_copy(block, 1, side_id).start()
                rows_copy(block, 0, mate_id).start()

            return inner

        def relay_side(way, inner):
            at_line, exists = place(step - 1, way)
            block = chip(at_line, 1 - side)

            @pl.when(exists)
            def _():
                rows_arrived(block, core)
                rows_copy(block, 0, mate_id).start()

            return inner

        lax.fori_loop(0, 2, relay_line, 0)
        lax.fori_loop(0, 2, relay_side, 0)

        @pl.when(step == 0)
        def _():
            for load in loads:
                load.wait()

        def compute(index, inner):
            way = index % 2
            mine = index // 2
            at_line, exists = place(step - mine, way)
            block = chip(at_line, jnp.where(mine == 0, side, 1 - side))

            @pl.when(exists)
            def _():
                rows_arrived(block, other)
                expert(block)

            return inner

        lax.fori_loop(0, 4, compute, 0)
        return carry

    lax.fori_loop(0, depth + 1, gather_step, 0)

    def side_step(index, carry):
        step = depth - 1 - index // 2
        at_line, exists = place(step, index % 2)
        block = chip(at_line, 1 - side)

        @pl.when(exists)
        def _():
            mate_copy(block).wait_recv()
            total = part_buf[block, core].astype(jnp.float32) + mate_buf[block].astype(jnp.float32)
            part_buf[block, core] = total.astype(jnp.bfloat16)
            side_copy(at_line).start()

        return carry

    lax.fori_loop(0, 2 * depth, side_step, 0)

    def line_total(at_line):
        block = chip(at_line, side)
        mate_copy(block).wait_recv()
        side_copy(at_line).wait_recv()
        total = part_buf[block, core].astype(jnp.float32) + mate_buf[block].astype(jnp.float32)
        return total + side_buf[at_line].astype(jnp.float32)

    def line_step(index, carry):
        step = depth - 1 - index // 2
        at_line, exists = place(step, index % 2)
        block = chip(at_line, side)

        @pl.when(exists)
        def _():
            upward = at_line > line
            way = jnp.where(upward, 0, 1)
            feeds = jnp.where(upward, has_down, has_up)

            part_buf[block, core] = line_total(at_line).astype(jnp.bfloat16)

            @pl.when(feeds)
            def _():
                line_copy(at_line, way, up_id).wait_recv()
                total = part_buf[block, core].astype(jnp.float32)
                total = total + line_buf[way, at_line].astype(jnp.float32)
                part_buf[block, core] = total.astype(jnp.bfloat16)

            @pl.when(upward)
            def _():
                line_copy(at_line, 0, up_id).start()

            @pl.when(jnp.logical_not(upward))
            def _():
                line_copy(at_line, 1, down_id).start()

        return carry

    lax.fori_loop(0, 2 * (depth - 1), line_step, 0)

    hidden_ref[...] = hidden_ref[...] + line_total(line)

    @pl.when(has_down)
    def _():
        line_copy(line, 0, up_id).wait_recv()
        hidden_ref[...] = hidden_ref[...] + line_buf[0, line].astype(jnp.float32)

    @pl.when(has_up)
    def _():
        line_copy(line, 1, up_id).wait_recv()
        hidden_ref[...] = hidden_ref[...] + line_buf[1, line].astype(jnp.float32)

    out_ref[...] = hidden_ref[...].astype(out_ref.dtype)

    def drain(at_line, carry):
        block = chip(at_line, side)
        across = chip(at_line, 1 - side)
        rows_copy(block, 0, mate_id).wait_send()
        rows_copy(block, 1, side_id).wait_send()
        rows_copy(across, 0, mate_id).wait_send()

        @pl.when(has_up & (at_line <= line))
        def _():
            rows_copy(block, 2, up_id).wait_send()

        @pl.when(has_down & (at_line >= line))
        def _():
            rows_copy(block, 3, down_id).wait_send()

        mate_copy(block).wait_send()
        mate_copy(across).wait_send()
        side_copy(at_line).wait_send()

        @pl.when(at_line != line)
        def _():
            line_copy(at_line, 0, up_id).wait_send()

        return carry

    lax.fori_loop(0, depth, drain, 0)


def routed_experts(rows, hidden_state, w_gate, w_up, w_down):
    experts = lax.axis_size("att")
    depth = experts // INNER
    tokens, padded = rows.shape
    width = hidden_state.shape[1]
    inner = w_gate.shape[2]
    bf16 = jnp.bfloat16
    dma = pltpu.SemaphoreType.DMA
    vmem = pl.BlockSpec(memory_space=pltpu.VMEM)
    hbm = pl.BlockSpec(memory_space=pl.ANY)

    def body(*refs):
        x_ref, hidden_in, *rest = refs
        hidden = rest[-1]
        hidden[...] = hidden_in[...]
        moe_kernel(depth, x_ref, hidden, *rest[:-1])

    return pl.pallas_call(
        body,
        out_shape=jax.ShapeDtypeStruct((tokens, width), bf16),
        in_specs=[vmem, vmem, hbm, hbm, hbm],
        out_specs=vmem,
        scratch_shapes=[
            pltpu.VMEM((experts, 2, tokens, padded), bf16),
            pltpu.VMEM((experts, 2, tokens, width), bf16),
            pltpu.VMEM((experts, tokens, width), bf16),
            pltpu.VMEM((depth, tokens, width), bf16),
            pltpu.VMEM((2, depth, tokens, width), bf16),
            pltpu.VMEM((width, inner), bf16),
            pltpu.VMEM((width, inner), bf16),
            pltpu.VMEM((inner, width), bf16),
            dma((3,)),
            dma,
            dma((experts, 4)),
            dma((experts, 2)),
            dma((experts,)),
            dma((experts,)),
            dma((depth,)),
            dma((depth,)),
            dma((depth,)),
            dma((2, depth)),
            pltpu.VMEM((tokens, width), jnp.float32),
        ],
        compiler_params=pltpu.CompilerParams(
            collective_id=0, has_side_effects=True, vmem_limit_bytes=62 * 1024 * 1024
        ),
    )(rows, hidden_state, w_gate, w_up, w_down)


def per_device(
    query,
    new_key,
    new_value,
    cache_keys,
    cache_values,
    lengths,
    out_proj,
    residual,
    norm_gain,
    router,
    routes,
    w_gate,
    w_up,
    w_down,
):
    attended = attend(query, new_key, new_value, cache_keys, cache_values, lengths)
    summed = lax.psum_scatter(
        jnp.dot(attended, out_proj, preferred_element_type=jnp.float32),
        "exp",
        scatter_dimension=0,
        tiled=True,
    )
    hidden_state = residual.astype(jnp.float32) + summed
    mean_square = jnp.mean(hidden_state * hidden_state, axis=-1, keepdims=True)
    normed = (hidden_state * lax.rsqrt(mean_square + 1e-05) * norm_gain).astype(jnp.bfloat16)
    logits = jnp.dot(normed.astype(jnp.float32), router, precision=lax.Precision.HIGHEST)
    experts = lax.axis_size("att")
    named = jnp.any(routes[:, :, None] == jnp.arange(experts)[None, None, :], axis=1)
    squashed = jnp.where(named, jax.nn.sigmoid(logits), 0.0)
    gate_weights = squashed / jnp.sum(squashed, axis=1, keepdims=True)
    coarse = lax.reduce_precision(gate_weights, 8, 7)
    fine = (gate_weights - coarse).astype(jnp.bfloat16)
    width = normed.shape[1]
    spare = pl.cdiv(width + 2 * experts, 128) * 128 - width - 2 * experts
    rows = jnp.concatenate(
        [normed, coarse.astype(jnp.bfloat16), fine, jnp.zeros((normed.shape[0], spare), jnp.bfloat16)],
        axis=1,
    )
    return routed_experts(rows, hidden_state, w_gate, w_up, w_down)


def solution(mesh):
    in_specs = (
        P(("groups", "att"), "exp"),
        P(("groups", "att"), "exp"),
        P(("groups", "att"), "exp"),
        P(("groups", "att"), None, "exp"),
        P(("groups", "att"), None, "exp"),
        P(("groups", "att")),
        P("exp", None),
        P(("groups", "att", "exp"), None),
        P(),
        P(),
        P(("groups", "att", "exp"), None),
        P("att", None, "exp"),
        P("att", None, "exp"),
        P("att", "exp", None),
    )
    out_specs = P(("groups", "att", "exp"), None)
    return jax.shard_map(
        per_device, mesh=mesh, in_specs=in_specs, out_specs=out_specs, check_vma=False
    )
```

```python
import math

import jax
import jax.numpy as jnp
from jax import lax
from jax.experimental import pallas as pl
from jax.experimental.pallas import tpu as pltpu
from jax.sharding import PartitionSpec as P

HEAD = 64
INNER = 2


def dot_t(left, right):
    return lax.dot_general(left, right, (((1,), (1,)), ((), ())), preferred_element_type=jnp.float32)


def moe_kernel(
    depth,
    x_ref,
    hidden_ref,
    gate_hbm,
    up_hbm,
    down_hbm,
    out_ref,
    rows_buf,
    part_buf,
    mate_buf,
    side_buf,
    line_buf,
    gate_w,
    up_w,
    down_w,
    weight_sem,
    local_sem,
    rows_send,
    rows_recv,
    mate_send,
    mate_recv,
    side_send,
    side_recv,
    line_send,
    line_recv,
):
    me = lax.axis_index("att")
    core = lax.axis_index("exp")
    other = 1 - core
    line = me // INNER
    side = me % INNER
    width = hidden_ref.shape[1]
    experts = rows_buf.shape[0]
    tokens = x_ref.shape[0]
    padded = x_ref.shape[1]

    def chip(at_line, at_side):
        return at_line * INNER + at_side

    mate_id = {"exp": other}
    side_id = {"att": chip(line, 1 - side)}
    up_id = {"att": chip(jnp.minimum(line + 1, depth - 1), side)}
    down_id = {"att": chip(jnp.maximum(line - 1, 0), side)}
    has_up = line + 1 < depth
    has_down = line >= 1
    mesh_ids = pl.DeviceIdType.MESH

    barrier = pltpu.get_barrier_semaphore()
    pl.semaphore_signal(barrier, inc=1, device_id=mate_id, device_id_type=mesh_ids)
    pl.semaphore_signal(barrier, inc=1, device_id=side_id, device_id_type=mesh_ids)

    @pl.when(has_up)
    def _():
        pl.semaphore_signal(barrier, inc=1, device_id=up_id, device_id_type=mesh_ids)

    @pl.when(has_down)
    def _():
        pl.semaphore_signal(barrier, inc=1, device_id=down_id, device_id_type=mesh_ids)

    loads = [
        pltpu.make_async_copy(gate_hbm.at[0], gate_w, weight_sem.at[0]),
        pltpu.make_async_copy(up_hbm.at[0], up_w, weight_sem.at[1]),
        pltpu.make_async_copy(down_hbm.at[0], down_w, weight_sem.at[2]),
    ]
    own_copy = pltpu.make_async_copy(x_ref, rows_buf.at[me, core], local_sem)
    own_copy.start()
    for load in loads:
        load.start()
    own_copy.wait()
    pl.semaphore_wait(barrier, 2 + has_up.astype(jnp.int32) + has_down.astype(jnp.int32))

    def rows_copy(block, kind, target):
        return pltpu.make_async_remote_copy(
            src_ref=rows_buf.at[block, core],
            dst_ref=rows_buf.at[block, core],
            send_sem=rows_send.at[block, kind],
            recv_sem=rows_recv.at[block, core],
            device_id=target,
            device_id_type=mesh_ids,
        )

    def rows_arrived(block, lane):
        pltpu.make_async_remote_copy(
            src_ref=rows_buf.at[block, lane],
            dst_ref=rows_buf.at[block, lane],
            send_sem=rows_send.at[block, 0],
            recv_sem=rows_recv.at[block, lane],
            device_id=mate_id,
            device_id_type=mesh_ids,
        ).wait_recv()

    def mate_copy(block):
        return pltpu.make_async_remote_copy(
            src_ref=part_buf.at[block, other],
            dst_ref=mate_buf.at[block],
            send_sem=mate_send.at[block],
            recv_sem=mate_recv.at[block],
            device_id=mate_id,
            device_id_type=mesh_ids,
        )

    def side_copy(at_line):
        return pltpu.make_async_remote_copy(
            src_ref=part_buf.at[chip(at_line, 1 - side), core],
            dst_ref=side_buf.at[at_line],
            send_sem=side_send.at[at_line],
            recv_sem=side_recv.at[at_line],
            device_id=side_id,
            device_id_type=mesh_ids,
        )

    def line_copy(at_line, way, target):
        return pltpu.make_async_remote_copy(
            src_ref=part_buf.at[chip(at_line, side), core],
            dst_ref=line_buf.at[way, at_line],
            send_sem=line_send.at[at_line],
            recv_sem=line_recv.at[way, at_line],
            device_id=target,
            device_id_type=mesh_ids,
        )

    def place(step, way):
        at_line = jnp.where(way == 0, line - step, line + step)
        exists = (at_line >= 0) & (at_line < depth) & ((step > 0) | (way == 0))
        exists = exists & (step >= 0) & (step < depth)
        return jnp.clip(at_line, 0, depth - 1), exists

    def expert(block):
        rows = rows_buf[block].reshape(2 * tokens, padded)
        values = rows[:, :width]
        first = (width // 128) * 128
        tail = rows[:, first:].astype(jnp.float32)
        lanes = lax.broadcasted_iota(jnp.int32, tail.shape, 1) + first - width
        chosen = (lanes == me) | (lanes == me + experts)
        weight = jnp.sum(jnp.where(chosen, tail, 0.0), axis=1, keepdims=True)
        gate = dot_t(values, gate_w[...])
        up = dot_t(values, up_w[...])
        activated = (gate / (1.0 + jnp.exp(-gate)) * up).astype(jnp.bfloat16)
        result = jnp.dot(activated, down_w[...], preferred_element_type=jnp.float32)
        result = (result * weight).astype(jnp.bfloat16)
        part_buf[block] = result.reshape(2, tokens, width)
        mate_copy(block).start()

    def gather_step(step, carry):
        def relay_line(way, inner):
            at_line, exists = place(step, way)
            block = chip(at_line, side)

            @pl.when(exists)
            def _():
                @pl.when(step > 0)
                def _():
                    rows_arrived(block, core)

                @pl.when(has_up & (at_line <= line))
                def _():
                    rows_copy(block, 2, up_id).start()

                @pl.when(has_down & (at_line >= line))
                def _():
                    rows_copy(block, 3, down_id).start()

                rows_copy(block, 1, side_id).start()
                rows_copy(block, 0, mate_id).start()

            return inner

        def relay_side(way, inner):
            at_line, exists = place(step - 1, way)
            block = chip(at_line, 1 - side)

            @pl.when(exists)
            def _():
                rows_arrived(block, core)
                rows_copy(block, 0, mate_id).start()

            return inner

        lax.fori_loop(0, 2, relay_line, 0)
        lax.fori_loop(0, 2, relay_side, 0)

        @pl.when(step == 0)
        def _():
            for load in loads:
                load.wait()

        def compute(index, inner):
            way = index % 2
            mine = index // 2
            at_line, exists = place(step - mine, way)
            block = chip(at_line, jnp.where(mine == 0, side, 1 - side))

            @pl.when(exists)
            def _():
                rows_arrived(block, other)
                expert(block)

            return inner

        lax.fori_loop(0, 4, compute, 0)
        return carry

    lax.fori_loop(0, depth + 1, gather_step, 0)

    def side_step(index, carry):
        step = depth - 1 - index // 2
        at_line, exists = place(step, index % 2)
        block = chip(at_line, 1 - side)

        @pl.when(exists)
        def _():
            mate_copy(block).wait_recv()
            total = part_buf[block, core].astype(jnp.float32) + mate_buf[block].astype(jnp.float32)
            part_buf[block, core] = total.astype(jnp.bfloat16)
            side_copy(at_line).start()

        return carry

    lax.fori_loop(0, 2 * depth, side_step, 0)

    def line_total(at_line):
        block = chip(at_line, side)
        mate_copy(block).wait_recv()
        side_copy(at_line).wait_recv()
        total = part_buf[block, core].astype(jnp.float32) + mate_buf[block].astype(jnp.float32)
        return total + side_buf[at_line].astype(jnp.float32)

    def line_step(index, carry):
        step = depth - 1 - index // 2
        at_line, exists = place(step, index % 2)
        block = chip(at_line, side)

        @pl.when(exists)
        def _():
            upward = at_line > line
            way = jnp.where(upward, 0, 1)
            feeds = jnp.where(upward, has_down, has_up)

            part_buf[block, core] = line_total(at_line).astype(jnp.bfloat16)

            @pl.when(feeds)
            def _():
                line_copy(at_line, way, up_id).wait_recv()
                total = part_buf[block, core].astype(jnp.float32)
                total = total + line_buf[way, at_line].astype(jnp.float32)
                part_buf[block, core] = total.astype(jnp.bfloat16)

            @pl.when(upward)
            def _():
                line_copy(at_line, 0, up_id).start()

            @pl.when(jnp.logical_not(upward))
            def _():
                line_copy(at_line, 1, down_id).start()

        return carry

    lax.fori_loop(0, 2 * (depth - 1), line_step, 0)

    hidden_ref[...] = hidden_ref[...] + line_total(line)

    @pl.when(has_down)
    def _():
        line_copy(line, 0, up_id).wait_recv()
        hidden_ref[...] = hidden_ref[...] + line_buf[0, line].astype(jnp.float32)

    @pl.when(has_up)
    def _():
        line_copy(line, 1, up_id).wait_recv()
        hidden_ref[...] = hidden_ref[...] + line_buf[1, line].astype(jnp.float32)

    out_ref[...] = hidden_ref[...].astype(out_ref.dtype)

    def drain(at_line, carry):
        block = chip(at_line, side)
        across = chip(at_line, 1 - side)
        rows_copy(block, 0, mate_id).wait_send()
        rows_copy(block, 1, side_id).wait_send()
        rows_copy(across, 0, mate_id).wait_send()

        @pl.when(has_up & (at_line <= line))
        def _():
            rows_copy(block, 2, up_id).wait_send()

        @pl.when(has_down & (at_line >= line))
        def _():
            rows_copy(block, 3, down_id).wait_send()

        mate_copy(block).wait_send()
        mate_copy(across).wait_send()
        side_copy(at_line).wait_send()

        @pl.when(at_line != line)
        def _():
            line_copy(at_line, 0, up_id).wait_send()

        return carry

    lax.fori_loop(0, depth, drain, 0)


def routed_experts(rows, hidden_state, w_gate, w_up, w_down):
    experts = lax.axis_size("att")
    depth = experts // INNER
    tokens, padded = rows.shape
    width = hidden_state.shape[1]
    inner = w_gate.shape[2]
    bf16 = jnp.bfloat16
    dma = pltpu.SemaphoreType.DMA
    vmem = pl.BlockSpec(memory_space=pltpu.VMEM)
    hbm = pl.BlockSpec(memory_space=pl.ANY)

    def body(*refs):
        x_ref, hidden_in, *rest = refs
        hidden = rest[-1]
        hidden[...] = hidden_in[...]
        moe_kernel(depth, x_ref, hidden, *rest[:-1])

    return pl.pallas_call(
        body,
        out_shape=jax.ShapeDtypeStruct((tokens, width), bf16),
        in_specs=[vmem, vmem, hbm, hbm, hbm],
        out_specs=vmem,
        scratch_shapes=[
            pltpu.VMEM((experts, 2, tokens, padded), bf16),
            pltpu.VMEM((experts, 2, tokens, width), bf16),
            pltpu.VMEM((experts, tokens, width), bf16),
            pltpu.VMEM((depth, tokens, width), bf16),
            pltpu.VMEM((2, depth, tokens, width), bf16),
            pltpu.VMEM((inner, width), bf16),
            pltpu.VMEM((inner, width), bf16),
            pltpu.VMEM((inner, width), bf16),
            dma((3,)),
            dma,
            dma((experts, 4)),
            dma((experts, 2)),
            dma((experts,)),
            dma((experts,)),
            dma((depth,)),
            dma((depth,)),
            dma((depth,)),
            dma((2, depth)),
            pltpu.VMEM((tokens, width), jnp.float32),
        ],
        compiler_params=pltpu.CompilerParams(
            collective_id=0, has_side_effects=True, vmem_limit_bytes=62 * 1024 * 1024
        ),
    )(rows, hidden_state, jnp.swapaxes(w_gate, 1, 2), jnp.swapaxes(w_up, 1, 2), w_down)


def attend_block(query, new_key, new_value, keys, values, lengths):
    rows = query.shape[0]
    heads = query.shape[1] // HEAD
    lane_heads = new_key.shape[1] // HEAD
    group = heads // lane_heads
    cache_len = keys.shape[1]
    pair = 2 * HEAD
    inverse_root = 1.0 / math.sqrt(HEAD)
    lanes = lax.broadcasted_iota(jnp.int32, (rows, pair), 1)
    low = lanes < HEAD
    pieces = []
    for head in range(heads):
        tile = query[:, (head // 2) * pair : (head // 2 + 1) * pair]
        lane_head = head // group
        if head % 2 != lane_head:
            tile = pltpu.roll(tile, HEAD, 1)
        pieces.append(jnp.where(low if lane_head == 0 else jnp.logical_not(low), tile, 0.0))
    stacked = jnp.concatenate(pieces, axis=0)
    tall_key = jnp.concatenate([new_key] * heads, axis=0)
    tall_value = jnp.concatenate([new_value] * heads, axis=0)
    tall_length = jnp.concatenate([lengths] * heads, axis=0)
    fresh = jnp.sum(stacked * tall_key, axis=1, keepdims=True) * inverse_root
    scores = dot_t(stacked.astype(jnp.bfloat16), keys.reshape(rows * cache_len, pair)) * inverse_root
    position = lax.broadcasted_iota(jnp.int32, scores.shape, 1)
    row = lax.broadcasted_iota(jnp.int32, (scores.shape[0], 1), 0)
    start = (row % rows) * cache_len
    live = (position >= start) & (position < start + tall_length)
    scores = jnp.where(live, scores, -1e30)
    highest = jnp.maximum(jnp.max(scores, axis=1, keepdims=True), fresh)
    cached_exp = jnp.exp(scores - highest)
    fresh_exp = jnp.exp(fresh - highest)
    scale = 1.0 / (jnp.sum(cached_exp, axis=1, keepdims=True) + fresh_exp)
    probs = (cached_exp * scale).astype(jnp.bfloat16)
    fresh_probs = (fresh_exp * scale).astype(jnp.bfloat16).astype(jnp.float32)
    output = jnp.dot(
        probs, values.reshape(rows * cache_len, pair), preferred_element_type=jnp.float32
    )
    output = output + fresh_probs * tall_value
    tiles = []
    for at in range(heads // 2):
        first = output[2 * at * rows : (2 * at + 1) * rows]
        second = output[(2 * at + 1) * rows : (2 * at + 2) * rows]
        if (2 * at) // group == 0:
            second = pltpu.roll(second, HEAD, 1)
        else:
            first = pltpu.roll(first, HEAD, 1)
        tiles.append(jnp.where(low, first, second))
    return jnp.concatenate(tiles, axis=1)


STEP = 16
HALF = 8
SPAN = 768


def attention_kernel(
    experts,
    query_ref,
    new_key_ref,
    new_value_ref,
    lengths_ref,
    residual_ref,
    gain_ref,
    router_ref,
    routes_ref,
    keys_hbm,
    values_hbm,
    proj_hbm,
    rows_ref,
    hidden_ref,
    keys_buf,
    values_buf,
    proj_w,
    attended,
    sent,
    landed,
    wide_router,
    keys_sem,
    values_sem,
    proj_sem,
    send_sem,
    recv_sem,
):
    core = lax.axis_index("exp")
    other = 1 - core
    mate = {"exp": other}
    barrier = pltpu.get_barrier_semaphore()
    pl.semaphore_signal(barrier, inc=1, device_id=mate, device_id_type=pl.DeviceIdType.MESH)
    requests = query_ref.shape[0]
    tokens, width = residual_ref.shape
    steps = requests // STEP

    def cache_load(step):
        span = pl.ds(step * STEP, STEP)
        return (
            pltpu.make_async_copy(keys_hbm.at[span], keys_buf.at[span], keys_sem.at[step]),
            pltpu.make_async_copy(values_hbm.at[span], values_buf.at[span], values_sem.at[step]),
        )

    proj_load = pltpu.make_async_copy(proj_hbm, proj_w, proj_sem)
    for step in range(steps):
        for load in cache_load(step):
            load.start()
    proj_load.start()

    first = (width // 128) * 128
    base = width - first
    wide_router[...] = jnp.zeros_like(wide_router)
    wide_router[base : base + experts, :] = router_ref[...]
    wide_router[base + experts : base + 2 * experts, :] = router_ref[...]

    def attend_step(step, carry):
        span = pl.ds(pl.multiple_of(step * STEP, STEP), STEP)
        for load in cache_load(step):
            load.wait()
        query = query_ref[span, :].astype(jnp.float32)
        new_key = new_key_ref[span, :].astype(jnp.float32)
        new_value = new_value_ref[span, :].astype(jnp.float32)
        lengths = lengths_ref[span, :]
        keys = keys_buf[span]
        values = values_buf[span]
        parts = []
        for half in range(STEP // HALF):
            cut = slice(half * HALF, (half + 1) * HALF)
            parts.append(
                attend_block(
                    query[cut], new_key[cut], new_value[cut], keys[cut], values[cut], lengths[cut]
                )
            )
        attended[span, :] = jnp.concatenate(parts, axis=0).astype(jnp.bfloat16)
        return carry

    lax.fori_loop(0, steps, attend_step, 0)

    proj_load.wait()
    pl.semaphore_wait(barrier, 1)
    theirs = attended[pl.ds(pl.multiple_of(other * tokens, tokens), tokens), :]
    mine = attended[pl.ds(pl.multiple_of(core * tokens, tokens), tokens), :]
    both = jnp.concatenate([theirs, mine], axis=0)
    copies = []
    for at, begin in enumerate(range(0, width, SPAN)):
        end = min(begin + SPAN, width)
        product = dot_t(both, proj_w[begin:end, :])
        sent[at, :, : end - begin] = product[:tokens]
        copy = pltpu.make_async_remote_copy(
            src_ref=sent.at[at],
            dst_ref=landed.at[at],
            send_sem=send_sem.at[at],
            recv_sem=recv_sem.at[at],
            device_id=mate,
            device_id_type=pl.DeviceIdType.MESH,
        )
        copy.start()
        copies.append(copy)
        hidden_ref[:, begin:end] = (
            residual_ref[:, begin:end].astype(jnp.float32) + product[tokens:]
        )
    squares = jnp.zeros((tokens, 1), jnp.float32)
    for at, begin in enumerate(range(0, width, SPAN)):
        end = min(begin + SPAN, width)
        copies[at].wait_recv()
        total = hidden_ref[:, begin:end] + landed[at, :, : end - begin]
        hidden_ref[:, begin:end] = total
        squares = squares + jnp.sum(total * total, axis=1, keepdims=True)
    scale = lax.rsqrt(squares / width + 1e-05)
    normed = (hidden_ref[...] * scale * gain_ref[...]).astype(jnp.bfloat16)
    logits = lax.dot_general(
        normed.astype(jnp.float32),
        wide_router[...],
        (((1,), (1,)), ((), ())),
        precision=lax.Precision.HIGHEST,
        preferred_element_type=jnp.float32,
    )
    lane = lax.broadcasted_iota(jnp.int32, logits.shape, 1) - base
    coarse_lane = (lane >= 0) & (lane < experts)
    fine_lane = (lane >= experts) & (lane < 2 * experts)
    expert = jnp.where(fine_lane, lane - experts, lane)
    named = jnp.zeros(logits.shape, jnp.bool_)
    for at in range(routes_ref.shape[1]):
        named = named | (routes_ref[:, at : at + 1] == expert)
    squashed = jnp.where(named, 1.0 / (1.0 + jnp.exp(-logits)), 0.0)
    totals = jnp.sum(jnp.where(coarse_lane, squashed, 0.0), axis=1, keepdims=True)
    weight = squashed / totals
    coarse = weight.astype(jnp.bfloat16).astype(jnp.float32)
    tail = jnp.where(coarse_lane, coarse, jnp.where(fine_lane, weight - coarse, 0.0))
    rows_ref[:, :width] = normed
    rows_ref[:, width:] = tail[:, base:].astype(jnp.bfloat16)
    for copy in copies:
        copy.wait_send()


def attention_layer(
    query, new_key, new_value, cache_keys, cache_values, lengths, out_proj, residual, gain, router, routes
):
    experts = lax.axis_size("att")
    requests = query.shape[0]
    tokens, width = residual.shape
    padded = pl.cdiv(width + 2 * experts, 128) * 128
    spans = pl.cdiv(width, SPAN)
    vmem = pl.BlockSpec(memory_space=pltpu.VMEM)
    hbm = pl.BlockSpec(memory_space=pl.ANY)
    bf16 = jnp.bfloat16
    dma = pltpu.SemaphoreType.DMA

    def body(*refs):
        attention_kernel(experts, *refs)

    return pl.pallas_call(
        body,
        out_shape=(
            jax.ShapeDtypeStruct((tokens, padded), bf16),
            jax.ShapeDtypeStruct((tokens, width), jnp.float32),
        ),
        in_specs=[vmem] * 8 + [hbm] * 3,
        out_specs=(vmem, vmem),
        scratch_shapes=[
            pltpu.VMEM(cache_keys.shape, bf16),
            pltpu.VMEM(cache_values.shape, bf16),
            pltpu.VMEM((width, out_proj.shape[0]), bf16),
            pltpu.VMEM(query.shape, bf16),
            pltpu.VMEM((spans, tokens, SPAN), jnp.float32),
            pltpu.VMEM((spans, tokens, SPAN), jnp.float32),
            pltpu.VMEM((128, width), jnp.float32),
            dma((requests // STEP,)),
            dma((requests // STEP,)),
            dma,
            dma((spans,)),
            dma((spans,)),
        ],
        compiler_params=pltpu.CompilerParams(
            collective_id=1, has_side_effects=True, vmem_limit_bytes=62 * 1024 * 1024
        ),
    )(
        query,
        new_key,
        new_value,
        lengths[:, None],
        residual,
        gain[None, :],
        router.T,
        routes,
        cache_keys,
        cache_values,
        out_proj.T,
    )


def per_device(
    query,
    new_key,
    new_value,
    cache_keys,
    cache_values,
    lengths,
    out_proj,
    residual,
    norm_gain,
    router,
    routes,
    w_gate,
    w_up,
    w_down,
):
    rows, hidden_state = attention_layer(
        query,
        new_key,
        new_value,
        cache_keys,
        cache_values,
        lengths,
        out_proj,
        residual,
        norm_gain,
        router,
        routes,
    )
    return routed_experts(rows, hidden_state, w_gate, w_up, w_down)


def solution(mesh):
    in_specs = (
        P(("groups", "att"), "exp"),
        P(("groups", "att"), "exp"),
        P(("groups", "att"), "exp"),
        P(("groups", "att"), None, "exp"),
        P(("groups", "att"), None, "exp"),
        P(("groups", "att")),
        P("exp", None),
        P(("groups", "att", "exp"), None),
        P(),
        P(),
        P(("groups", "att", "exp"), None),
        P("att", None, "exp"),
        P("att", None, "exp"),
        P("att", "exp", None),
    )
    out_specs = P(("groups", "att", "exp"), None)
    return jax.shard_map(
        per_device, mesh=mesh, in_specs=in_specs, out_specs=out_specs, check_vma=False
    )
```

```python
import math

import jax
import jax.numpy as jnp
from jax import lax
from jax.experimental import pallas as pl
from jax.experimental.pallas import tpu as pltpu
from jax.sharding import PartitionSpec as P

HEAD = 64
INNER = 2
CHUNKS = 2


def dot_t(left, right):
    return lax.dot_general(left, right, (((1,), (1,)), ((), ())), preferred_element_type=jnp.float32)


def moe_kernel(
    depth,
    x_ref,
    hidden_ref,
    gate_hbm,
    up_hbm,
    down_hbm,
    out_ref,
    rows_buf,
    part_buf,
    mate_buf,
    side_buf,
    line_buf,
    gate_w,
    up_w,
    down_w,
    weight_sem,
    local_sem,
    rows_send,
    rows_recv,
    mate_send,
    mate_recv,
    side_send,
    side_recv,
    line_send,
    line_recv,
):
    me = lax.axis_index("att")
    core = lax.axis_index("exp")
    other = 1 - core
    line = me // INNER
    side = me % INNER
    width = hidden_ref.shape[1]
    experts = rows_buf.shape[0]
    tokens = x_ref.shape[0]
    padded = x_ref.shape[1]
    slab = tokens // CHUNKS

    def chip(at_line, at_side):
        return at_line * INNER + at_side

    mate_id = {"exp": other}
    side_id = {"att": chip(line, 1 - side)}
    up_id = {"att": chip(jnp.minimum(line + 1, depth - 1), side)}
    down_id = {"att": chip(jnp.maximum(line - 1, 0), side)}
    has_up = line + 1 < depth
    has_down = line >= 1
    mesh_ids = pl.DeviceIdType.MESH

    barrier = pltpu.get_barrier_semaphore()
    pl.semaphore_signal(barrier, inc=1, device_id=mate_id, device_id_type=mesh_ids)
    pl.semaphore_signal(barrier, inc=1, device_id=side_id, device_id_type=mesh_ids)

    @pl.when(has_up)
    def _():
        pl.semaphore_signal(barrier, inc=1, device_id=up_id, device_id_type=mesh_ids)

    @pl.when(has_down)
    def _():
        pl.semaphore_signal(barrier, inc=1, device_id=down_id, device_id_type=mesh_ids)

    loads = [
        pltpu.make_async_copy(gate_hbm.at[0], gate_w, weight_sem.at[0]),
        pltpu.make_async_copy(up_hbm.at[0], up_w, weight_sem.at[1]),
        pltpu.make_async_copy(down_hbm.at[0], down_w, weight_sem.at[2]),
    ]
    own_copy = pltpu.make_async_copy(x_ref, rows_buf.at[me, core], local_sem)
    own_copy.start()
    for load in loads:
        load.start()
    own_copy.wait()
    pl.semaphore_wait(barrier, 2 + has_up.astype(jnp.int32) + has_down.astype(jnp.int32))

    def rows_of(chunk):
        return pl.ds(pl.multiple_of(chunk * slab, slab), slab)

    def rows_copy(block, chunk, kind, target):
        return pltpu.make_async_remote_copy(
            src_ref=rows_buf.at[block, core, rows_of(chunk)],
            dst_ref=rows_buf.at[block, core, rows_of(chunk)],
            send_sem=rows_send.at[block, chunk, kind],
            recv_sem=rows_recv.at[block, chunk, core],
            device_id=target,
            device_id_type=mesh_ids,
        )

    def rows_arrived(block, chunk, lane):
        pltpu.make_async_remote_copy(
            src_ref=rows_buf.at[block, lane, rows_of(chunk)],
            dst_ref=rows_buf.at[block, lane, rows_of(chunk)],
            send_sem=rows_send.at[block, chunk, 0],
            recv_sem=rows_recv.at[block, chunk, lane],
            device_id=mate_id,
            device_id_type=mesh_ids,
        ).wait_recv()

    def mate_copy(block):
        return pltpu.make_async_remote_copy(
            src_ref=part_buf.at[block, other],
            dst_ref=mate_buf.at[block],
            send_sem=mate_send.at[block],
            recv_sem=mate_recv.at[block],
            device_id=mate_id,
            device_id_type=mesh_ids,
        )

    def side_copy(at_line, chunk):
        return pltpu.make_async_remote_copy(
            src_ref=part_buf.at[chip(at_line, 1 - side), core, rows_of(chunk)],
            dst_ref=side_buf.at[at_line, rows_of(chunk)],
            send_sem=side_send.at[at_line, chunk],
            recv_sem=side_recv.at[at_line, chunk],
            device_id=side_id,
            device_id_type=mesh_ids,
        )

    def line_copy(at_line, chunk, way, target):
        return pltpu.make_async_remote_copy(
            src_ref=part_buf.at[chip(at_line, side), core, rows_of(chunk)],
            dst_ref=line_buf.at[way, at_line, rows_of(chunk)],
            send_sem=line_send.at[at_line, chunk],
            recv_sem=line_recv.at[way, at_line, chunk],
            device_id=target,
            device_id_type=mesh_ids,
        )

    def place(step, way):
        at_line = jnp.where(way == 0, line - step, line + step)
        exists = (at_line >= 0) & (at_line < depth) & ((step > 0) | (way == 0))
        exists = exists & (step >= 0) & (step < depth)
        return jnp.clip(at_line, 0, depth - 1), exists

    def expert(block):
        rows = rows_buf[block].reshape(2 * tokens, padded)
        values = rows[:, :width]
        first = (width // 128) * 128
        tail = rows[:, first:].astype(jnp.float32)
        lanes = lax.broadcasted_iota(jnp.int32, tail.shape, 1) + first - width
        chosen = (lanes == me) | (lanes == me + experts)
        weight = jnp.sum(jnp.where(chosen, tail, 0.0), axis=1, keepdims=True)
        gate = dot_t(values, gate_w[...])
        up = dot_t(values, up_w[...])
        activated = (gate / (1.0 + jnp.exp(-gate)) * up).astype(jnp.bfloat16)
        result = jnp.dot(activated, down_w[...], preferred_element_type=jnp.float32)
        result = (result * weight).astype(jnp.bfloat16)
        part_buf[block] = result.reshape(2, tokens, width)
        mate_copy(block).start()

    def compute(step, mine):
        def one(way, carry):
            at_line, exists = place(step, way)
            block = chip(at_line, jnp.where(mine, side, 1 - side))

            @pl.when(exists)
            def _():
                for chunk in range(CHUNKS):
                    rows_arrived(block, chunk, other)
                expert(block)

            return carry

        lax.fori_loop(0, 2, one, 0)

    def side_sum(step):
        def one(way, carry):
            at_line, exists = place(step, way)
            block = chip(at_line, 1 - side)

            @pl.when(exists)
            def _():
                mate_copy(block).wait_recv()

                def part(chunk, inner):
                    span = rows_of(chunk)
                    total = part_buf[block, core, span].astype(jnp.float32)
                    total = total + mate_buf[block, span].astype(jnp.float32)
                    part_buf[block, core, span] = total.astype(jnp.bfloat16)
                    side_copy(at_line, chunk).start()
                    return inner

                lax.fori_loop(0, CHUNKS, part, 0)

            return carry

        lax.fori_loop(0, 2, one, 0)

    early = max(depth - 2, 0)

    def gather_step(index, carry):
        step = index // CHUNKS
        chunk = index % CHUNKS

        @pl.when(index == CHUNKS)
        def _():
            for load in loads:
                load.wait()

        @pl.when(index == (depth + 1) * CHUNKS + 1)
        def _():
            side_sum(early)

        compute(jnp.where(chunk == 0, step - 1, step - 2), chunk == 0)

        def relay_line(way, inner):
            at_line, exists = place(step, way)
            block = chip(at_line, side)

            @pl.when(exists)
            def _():
                @pl.when(step > 0)
                def _():
                    rows_arrived(block, chunk, core)

                @pl.when(has_up & (at_line <= line))
                def _():
                    rows_copy(block, chunk, 2, up_id).start()

                @pl.when(has_down & (at_line >= line))
                def _():
                    rows_copy(block, chunk, 3, down_id).start()

                rows_copy(block, chunk, 1, side_id).start()
                rows_copy(block, chunk, 0, mate_id).start()

            return inner

        def relay_side(way, inner):
            at_line, exists = place(step - 1, way)
            block = chip(at_line, 1 - side)

            @pl.when(exists)
            def _():
                rows_arrived(block, chunk, core)
                rows_copy(block, chunk, 0, mate_id).start()

            return inner

        lax.fori_loop(0, 2, relay_line, 0)
        lax.fori_loop(0, 2, relay_side, 0)
        return carry

    lax.fori_loop(0, (depth + 2) * CHUNKS, gather_step, 0)

    def side_step(index, carry):
        step = depth - 1 - index

        @pl.when(step != early)
        def _():
            side_sum(step)

        return carry

    lax.fori_loop(0, depth, side_step, 0)

    def line_total(at_line, chunk):
        block = chip(at_line, side)
        span = rows_of(chunk)
        side_copy(at_line, chunk).wait_recv()
        total = part_buf[block, core, span].astype(jnp.float32)
        total = total + mate_buf[block, span].astype(jnp.float32)
        return total + side_buf[at_line, span].astype(jnp.float32)

    def line_step(index, carry):
        step = depth - 1 - index // (2 * CHUNKS)
        chunk = index // 2 % CHUNKS
        at_line, exists = place(step, index % 2)
        block = chip(at_line, side)
        span = rows_of(chunk)

        @pl.when(exists)
        def _():
            upward = at_line > line
            way = jnp.where(upward, 0, 1)
            feeds = jnp.where(upward, has_down, has_up)

            @pl.when(chunk == 0)
            def _():
                mate_copy(block).wait_recv()

            part_buf[block, core, span] = line_total(at_line, chunk).astype(jnp.bfloat16)

            @pl.when(feeds)
            def _():
                line_copy(at_line, chunk, way, up_id).wait_recv()
                total = part_buf[block, core, span].astype(jnp.float32)
                total = total + line_buf[way, at_line, span].astype(jnp.float32)
                part_buf[block, core, span] = total.astype(jnp.bfloat16)

            @pl.when(upward)
            def _():
                line_copy(at_line, chunk, 0, up_id).start()

            @pl.when(jnp.logical_not(upward))
            def _():
                line_copy(at_line, chunk, 1, down_id).start()

        return carry

    lax.fori_loop(0, 2 * CHUNKS * (depth - 1), line_step, 0)

    mate_copy(me).wait_recv()

    def finish(chunk, carry):
        span = rows_of(chunk)
        for exists, way in ((has_down, 0), (has_up, 1)):

            @pl.when(exists)
            def _():
                line_copy(line, chunk, way, up_id).wait_recv()
                hidden_ref[span, :] = hidden_ref[span, :] + line_buf[way, line, span].astype(
                    jnp.float32
                )

        total = hidden_ref[span, :] + line_total(line, chunk)
        out_ref[span, :] = total.astype(out_ref.dtype)
        return carry

    lax.fori_loop(0, CHUNKS, finish, 0)

    def drain(at_line, carry):
        block = chip(at_line, side)
        across = chip(at_line, 1 - side)
        mate_copy(block).wait_send()
        mate_copy(across).wait_send()
        for chunk in range(CHUNKS):
            rows_copy(block, chunk, 0, mate_id).wait_send()
            rows_copy(block, chunk, 1, side_id).wait_send()
            rows_copy(across, chunk, 0, mate_id).wait_send()

            @pl.when(has_up & (at_line <= line))
            def _():
                rows_copy(block, chunk, 2, up_id).wait_send()

            @pl.when(has_down & (at_line >= line))
            def _():
                rows_copy(block, chunk, 3, down_id).wait_send()

            side_copy(at_line, chunk).wait_send()

            @pl.when(at_line != line)
            def _():
                line_copy(at_line, chunk, 0, up_id).wait_send()

        return carry

    lax.fori_loop(0, depth, drain, 0)


def routed_experts(rows, hidden_state, w_gate, w_up, w_down):
    experts = lax.axis_size("att")
    depth = experts // INNER
    tokens, padded = rows.shape
    width = hidden_state.shape[1]
    inner = w_gate.shape[2]
    bf16 = jnp.bfloat16
    dma = pltpu.SemaphoreType.DMA
    vmem = pl.BlockSpec(memory_space=pltpu.VMEM)
    hbm = pl.BlockSpec(memory_space=pl.ANY)

    def body(*refs):
        x_ref, hidden_in, *rest = refs
        hidden = rest[-1]
        hidden[...] = hidden_in[...]
        moe_kernel(depth, x_ref, hidden, *rest[:-1])

    return pl.pallas_call(
        body,
        out_shape=jax.ShapeDtypeStruct((tokens, width), bf16),
        in_specs=[vmem, vmem, hbm, hbm, hbm],
        out_specs=vmem,
        scratch_shapes=[
            pltpu.VMEM((experts, 2, tokens, padded), bf16),
            pltpu.VMEM((experts, 2, tokens, width), bf16),
            pltpu.VMEM((experts, tokens, width), bf16),
            pltpu.VMEM((depth, tokens, width), bf16),
            pltpu.VMEM((2, depth, tokens, width), bf16),
            pltpu.VMEM((inner, width), bf16),
            pltpu.VMEM((inner, width), bf16),
            pltpu.VMEM((inner, width), bf16),
            dma((3,)),
            dma,
            dma((experts, CHUNKS, 4)),
            dma((experts, CHUNKS, 2)),
            dma((experts,)),
            dma((experts,)),
            dma((depth, CHUNKS)),
            dma((depth, CHUNKS)),
            dma((depth, CHUNKS)),
            dma((2, depth, CHUNKS)),
            pltpu.VMEM((tokens, width), jnp.float32),
        ],
        compiler_params=pltpu.CompilerParams(
            collective_id=0, has_side_effects=True, vmem_limit_bytes=62 * 1024 * 1024
        ),
    )(rows, hidden_state, jnp.swapaxes(w_gate, 1, 2), jnp.swapaxes(w_up, 1, 2), w_down)


def attend_block(query, new_key, new_value, keys, values, lengths):
    rows = query.shape[0]
    heads = query.shape[1] // HEAD
    lane_heads = new_key.shape[1] // HEAD
    group = heads // lane_heads
    cache_len = keys.shape[1]
    pair = 2 * HEAD
    inverse_root = 1.0 / math.sqrt(HEAD)
    lanes = lax.broadcasted_iota(jnp.int32, (rows, pair), 1)
    low = lanes < HEAD
    pieces = []
    for head in range(heads):
        tile = query[:, (head // 2) * pair : (head // 2 + 1) * pair]
        lane_head = head // group
        if head % 2 != lane_head:
            tile = pltpu.roll(tile, HEAD, 1)
        pieces.append(jnp.where(low if lane_head == 0 else jnp.logical_not(low), tile, 0.0))
    stacked = jnp.concatenate(pieces, axis=0)
    tall_key = jnp.concatenate([new_key] * heads, axis=0)
    tall_value = jnp.concatenate([new_value] * heads, axis=0)
    fresh = jnp.sum(stacked * tall_key, axis=1, keepdims=True) * inverse_root
    scores = dot_t(stacked.astype(jnp.bfloat16), keys.reshape(rows * cache_len, pair)) * inverse_root
    position = lax.broadcasted_iota(jnp.int32, scores.shape, 1)
    row = lax.broadcasted_iota(jnp.int32, (scores.shape[0], 1), 0)
    request = row % rows
    start = request * cache_len
    tall_length = jnp.zeros_like(row)
    for at in range(rows):
        tall_length = jnp.where(request == at, lengths[at], tall_length)
    live = (position >= start) & (position < start + tall_length)
    scores = jnp.where(live, scores, -1e30)
    highest = jnp.maximum(jnp.max(scores, axis=1, keepdims=True), fresh)
    cached_exp = jnp.exp(scores - highest)
    fresh_exp = jnp.exp(fresh - highest)
    scale = 1.0 / (jnp.sum(cached_exp, axis=1, keepdims=True) + fresh_exp)
    probs = (cached_exp * scale).astype(jnp.bfloat16)
    fresh_probs = (fresh_exp * scale).astype(jnp.bfloat16).astype(jnp.float32)
    output = jnp.dot(
        probs, values.reshape(rows * cache_len, pair), preferred_element_type=jnp.float32
    )
    output = output + fresh_probs * tall_value
    tiles = []
    for at in range(heads // 2):
        first = output[2 * at * rows : (2 * at + 1) * rows]
        second = output[(2 * at + 1) * rows : (2 * at + 2) * rows]
        if (2 * at) // group == 0:
            second = pltpu.roll(second, HEAD, 1)
        else:
            first = pltpu.roll(first, HEAD, 1)
        tiles.append(jnp.where(low, first, second))
    return jnp.concatenate(tiles, axis=1)


STEP = 16
HALF = 8
SPAN = 768


def attention_kernel(
    experts,
    query_ref,
    new_key_ref,
    new_value_ref,
    lengths_ref,
    residual_ref,
    gain_ref,
    router_ref,
    routes_ref,
    keys_hbm,
    values_hbm,
    proj_hbm,
    rows_ref,
    hidden_ref,
    keys_buf,
    values_buf,
    proj_w,
    attended,
    sent,
    landed,
    wide_router,
    keys_sem,
    values_sem,
    proj_sem,
    send_sem,
    recv_sem,
):
    core = lax.axis_index("exp")
    other = 1 - core
    mate = {"exp": other}
    barrier = pltpu.get_barrier_semaphore()
    pl.semaphore_signal(barrier, inc=1, device_id=mate, device_id_type=pl.DeviceIdType.MESH)
    requests = query_ref.shape[0]
    tokens, width = residual_ref.shape
    steps = requests // STEP

    def cache_load(step):
        span = pl.ds(step * STEP, STEP)
        return (
            pltpu.make_async_copy(keys_hbm.at[span], keys_buf.at[span], keys_sem.at[step]),
            pltpu.make_async_copy(values_hbm.at[span], values_buf.at[span], values_sem.at[step]),
        )

    proj_load = pltpu.make_async_copy(proj_hbm, proj_w, proj_sem)
    for step in range(steps):
        for load in cache_load(step):
            load.start()
    proj_load.start()

    first = (width // 128) * 128
    base = width - first
    wide_router[...] = jnp.zeros_like(wide_router)
    wide_router[base : base + experts, :] = router_ref[...]
    wide_router[base + experts : base + 2 * experts, :] = router_ref[...]

    def attend_step(step, carry):
        span = pl.ds(pl.multiple_of(step * STEP, STEP), STEP)
        for load in cache_load(step):
            load.wait()
        query = query_ref[span, :].astype(jnp.float32)
        new_key = new_key_ref[span, :].astype(jnp.float32)
        new_value = new_value_ref[span, :].astype(jnp.float32)
        keys = keys_buf[span]
        values = values_buf[span]
        parts = []
        for half in range(STEP // HALF):
            cut = slice(half * HALF, (half + 1) * HALF)
            lengths = [lengths_ref[step * STEP + half * HALF + at] for at in range(HALF)]
            parts.append(
                attend_block(
                    query[cut], new_key[cut], new_value[cut], keys[cut], values[cut], lengths
                )
            )
        attended[span, :] = jnp.concatenate(parts, axis=0).astype(jnp.bfloat16)
        return carry

    lax.fori_loop(0, steps, attend_step, 0)

    proj_load.wait()
    pl.semaphore_wait(barrier, 1)
    theirs = attended[pl.ds(pl.multiple_of(other * tokens, tokens), tokens), :]
    mine = attended[pl.ds(pl.multiple_of(core * tokens, tokens), tokens), :]
    both = jnp.concatenate([theirs, mine], axis=0)
    copies = []
    for at, begin in enumerate(range(0, width, SPAN)):
        end = min(begin + SPAN, width)
        product = dot_t(both, proj_w[begin:end, :])
        sent[at, :, : end - begin] = product[:tokens]
        copy = pltpu.make_async_remote_copy(
            src_ref=sent.at[at],
            dst_ref=landed.at[at],
            send_sem=send_sem.at[at],
            recv_sem=recv_sem.at[at],
            device_id=mate,
            device_id_type=pl.DeviceIdType.MESH,
        )
        copy.start()
        copies.append(copy)
        hidden_ref[:, begin:end] = (
            residual_ref[:, begin:end].astype(jnp.float32) + product[tokens:]
        )
    squares = jnp.zeros((tokens, 1), jnp.float32)
    for at, begin in enumerate(range(0, width, SPAN)):
        end = min(begin + SPAN, width)
        copies[at].wait_recv()
        total = hidden_ref[:, begin:end] + landed[at, :, : end - begin]
        hidden_ref[:, begin:end] = total
        squares = squares + jnp.sum(total * total, axis=1, keepdims=True)
    scale = lax.rsqrt(squares / width + 1e-05)
    normed = (hidden_ref[...] * scale * gain_ref[...].reshape(1, width)).astype(jnp.bfloat16)
    logits = lax.dot_general(
        normed.astype(jnp.float32),
        wide_router[...],
        (((1,), (1,)), ((), ())),
        precision=lax.Precision.HIGHEST,
        preferred_element_type=jnp.float32,
    )
    lane = lax.broadcasted_iota(jnp.int32, logits.shape, 1) - base
    coarse_lane = (lane >= 0) & (lane < experts)
    fine_lane = (lane >= experts) & (lane < 2 * experts)
    column = lax.broadcasted_iota(jnp.int32, (logits.shape[1], 1), 0) - base
    column = jnp.where(column >= experts, column - experts, column)
    hits = jnp.zeros((logits.shape[1], tokens), jnp.float32)
    for at in range(routes_ref.shape[0]):
        hits = jnp.where(routes_ref[at : at + 1, :] == column, 1.0, hits)
    named = hits.T > 0.5
    squashed = jnp.where(named, 1.0 / (1.0 + jnp.exp(-logits)), 0.0)
    totals = jnp.sum(jnp.where(coarse_lane, squashed, 0.0), axis=1, keepdims=True)
    weight = squashed / totals
    coarse = weight.astype(jnp.bfloat16).astype(jnp.float32)
    tail = jnp.where(coarse_lane, coarse, jnp.where(fine_lane, weight - coarse, 0.0))
    rows_ref[:, :width] = normed
    rows_ref[:, width:] = tail[:, base:].astype(jnp.bfloat16)
    for copy in copies:
        copy.wait_send()


def attention_layer(
    query, new_key, new_value, cache_keys, cache_values, lengths, out_proj, residual, gain, router, routes
):
    experts = lax.axis_size("att")
    requests = query.shape[0]
    tokens, width = residual.shape
    padded = pl.cdiv(width + 2 * experts, 128) * 128
    spans = pl.cdiv(width, SPAN)
    vmem = pl.BlockSpec(memory_space=pltpu.VMEM)
    hbm = pl.BlockSpec(memory_space=pl.ANY)
    bf16 = jnp.bfloat16
    dma = pltpu.SemaphoreType.DMA

    def body(*refs):
        attention_kernel(experts, *refs)

    return pl.pallas_call(
        body,
        out_shape=(
            jax.ShapeDtypeStruct((tokens, padded), bf16),
            jax.ShapeDtypeStruct((tokens, width), jnp.float32),
        ),
        in_specs=[vmem] * 3 + [pl.BlockSpec(memory_space=pltpu.SMEM)] + [vmem] * 4 + [hbm] * 3,
        out_specs=(vmem, vmem),
        scratch_shapes=[
            pltpu.VMEM(cache_keys.shape, bf16),
            pltpu.VMEM(cache_values.shape, bf16),
            pltpu.VMEM((width, out_proj.shape[0]), bf16),
            pltpu.VMEM(query.shape, bf16),
            pltpu.VMEM((spans, tokens, SPAN), jnp.float32),
            pltpu.VMEM((spans, tokens, SPAN), jnp.float32),
            pltpu.VMEM((128, width), jnp.float32),
            dma((requests // STEP,)),
            dma((requests // STEP,)),
            dma,
            dma((spans,)),
            dma((spans,)),
        ],
        compiler_params=pltpu.CompilerParams(
            collective_id=1, has_side_effects=True, vmem_limit_bytes=62 * 1024 * 1024
        ),
    )(
        query,
        new_key,
        new_value,
        lengths,
        residual,
        gain,
        router.T,
        routes.T,
        cache_keys,
        cache_values,
        out_proj.T,
    )


def per_device(
    query,
    new_key,
    new_value,
    cache_keys,
    cache_values,
    lengths,
    out_proj,
    residual,
    norm_gain,
    router,
    routes,
    w_gate,
    w_up,
    w_down,
):
    rows, hidden_state = attention_layer(
        query,
        new_key,
        new_value,
        cache_keys,
        cache_values,
        lengths,
        out_proj,
        residual,
        norm_gain,
        router,
        routes,
    )
    return routed_experts(rows, hidden_state, w_gate, w_up, w_down)


def solution(mesh):
    in_specs = (
        P(("groups", "att"), "exp"),
        P(("groups", "att"), "exp"),
        P(("groups", "att"), "exp"),
        P(("groups", "att"), None, "exp"),
        P(("groups", "att"), None, "exp"),
        P(("groups", "att")),
        P("exp", None),
        P(("groups", "att", "exp"), None),
        P(),
        P(),
        P(("groups", "att", "exp"), None),
        P("att", None, "exp"),
        P("att", None, "exp"),
        P("att", "exp", None),
    )
    out_specs = P(("groups", "att", "exp"), None)
    return jax.shard_map(
        per_device, mesh=mesh, in_specs=in_specs, out_specs=out_specs, check_vma=False
    )
```

```python
import math

import jax
import jax.numpy as jnp
from jax import lax
from jax.experimental import pallas as pl
from jax.experimental.pallas import tpu as pltpu
from jax.sharding import PartitionSpec as P

HEAD = 64
INNER = 2
CHUNKS = 2


def dot_t(left, right):
    return lax.dot_general(left, right, (((1,), (1,)), ((), ())), preferred_element_type=jnp.float32)


def moe_kernel(
    depth,
    x_ref,
    hidden_ref,
    gate_hbm,
    up_hbm,
    down_hbm,
    out_ref,
    rows_buf,
    part_buf,
    mate_buf,
    side_buf,
    line_buf,
    gate_w,
    up_w,
    down_w,
    weight_sem,
    local_sem,
    rows_send,
    rows_recv,
    mate_send,
    mate_recv,
    side_send,
    side_recv,
    line_send,
    line_recv,
    far_buf,
    far_send,
    far_recv,
):
    me = lax.axis_index("att")
    core = lax.axis_index("exp")
    other = 1 - core
    line = me // INNER
    side = me % INNER
    width = hidden_ref.shape[1]
    experts = rows_buf.shape[0]
    tokens = x_ref.shape[0]
    padded = x_ref.shape[1]
    slab = tokens // CHUNKS

    def chip(at_line, at_side):
        return at_line * INNER + at_side

    mate_id = {"exp": other}
    side_id = {"att": chip(line, 1 - side)}
    up_id = {"att": chip(jnp.minimum(line + 1, depth - 1), side)}
    down_id = {"att": chip(jnp.maximum(line - 1, 0), side)}
    has_up = line + 1 < depth
    has_down = line >= 1
    mesh_ids = pl.DeviceIdType.MESH

    barrier = pltpu.get_barrier_semaphore()
    pl.semaphore_signal(barrier, inc=1, device_id=mate_id, device_id_type=mesh_ids)
    pl.semaphore_signal(barrier, inc=1, device_id=side_id, device_id_type=mesh_ids)

    @pl.when(has_up)
    def _():
        pl.semaphore_signal(barrier, inc=1, device_id=up_id, device_id_type=mesh_ids)

    @pl.when(has_down)
    def _():
        pl.semaphore_signal(barrier, inc=1, device_id=down_id, device_id_type=mesh_ids)

    loads = [
        pltpu.make_async_copy(gate_hbm.at[0], gate_w, weight_sem.at[0]),
        pltpu.make_async_copy(up_hbm.at[0], up_w, weight_sem.at[1]),
        pltpu.make_async_copy(down_hbm.at[0], down_w, weight_sem.at[2]),
    ]
    own_copy = pltpu.make_async_copy(x_ref, rows_buf.at[me, core], local_sem)
    own_copy.start()
    for load in loads:
        load.start()
    own_copy.wait()
    pl.semaphore_wait(barrier, 2 + has_up.astype(jnp.int32) + has_down.astype(jnp.int32))

    def crosses_first(at_line, chunk):
        return ((at_line == 0) | (at_line == depth - 1)) & (chunk == CHUNKS - 1)

    def rows_of(chunk):
        return pl.ds(pl.multiple_of(chunk * slab, slab), slab)

    def rows_copy(block, chunk, kind, target):
        return pltpu.make_async_remote_copy(
            src_ref=rows_buf.at[block, core, rows_of(chunk)],
            dst_ref=rows_buf.at[block, core, rows_of(chunk)],
            send_sem=rows_send.at[block, chunk, kind],
            recv_sem=rows_recv.at[block, chunk, core],
            device_id=target,
            device_id_type=mesh_ids,
        )

    def rows_arrived(block, chunk, lane):
        pltpu.make_async_remote_copy(
            src_ref=rows_buf.at[block, lane, rows_of(chunk)],
            dst_ref=rows_buf.at[block, lane, rows_of(chunk)],
            send_sem=rows_send.at[block, chunk, 0],
            recv_sem=rows_recv.at[block, chunk, lane],
            device_id=mate_id,
            device_id_type=mesh_ids,
        ).wait_recv()

    def mate_copy(block):
        return pltpu.make_async_remote_copy(
            src_ref=part_buf.at[block, other],
            dst_ref=mate_buf.at[block],
            send_sem=mate_send.at[block],
            recv_sem=mate_recv.at[block],
            device_id=mate_id,
            device_id_type=mesh_ids,
        )

    def side_copy(at_line, chunk):
        return pltpu.make_async_remote_copy(
            src_ref=part_buf.at[chip(at_line, 1 - side), core, rows_of(chunk)],
            dst_ref=side_buf.at[at_line, rows_of(chunk)],
            send_sem=side_send.at[at_line, chunk],
            recv_sem=side_recv.at[at_line, chunk],
            device_id=side_id,
            device_id_type=mesh_ids,
        )

    def far_copy(at_line, way, target):
        return pltpu.make_async_remote_copy(
            src_ref=part_buf.at[chip(at_line, 1 - side), core, rows_of(CHUNKS - 1)],
            dst_ref=far_buf.at[way],
            send_sem=far_send.at[way],
            recv_sem=far_recv.at[way],
            device_id=target,
            device_id_type=mesh_ids,
        )

    def far_add(at_line, way):
        far_copy(at_line, way, up_id).wait_recv()
        across = chip(at_line, 1 - side)
        span = rows_of(CHUNKS - 1)
        total = part_buf[across, core, span].astype(jnp.float32)
        total = total + far_buf[way].astype(jnp.float32)
        part_buf[across, core, span] = total.astype(jnp.bfloat16)

    def line_copy(at_line, chunk, way, target):
        return pltpu.make_async_remote_copy(
            src_ref=part_buf.at[chip(at_line, side), core, rows_of(chunk)],
            dst_ref=line_buf.at[way, at_line, rows_of(chunk)],
            send_sem=line_send.at[at_line, chunk],
            recv_sem=line_recv.at[way, at_line, chunk],
            device_id=target,
            device_id_type=mesh_ids,
        )

    def place(step, way):
        at_line = jnp.where(way == 0, line - step, line + step)
        exists = (at_line >= 0) & (at_line < depth) & ((step > 0) | (way == 0))
        exists = exists & (step >= 0) & (step < depth)
        return jnp.clip(at_line, 0, depth - 1), exists

    def expert(block):
        rows = rows_buf[block].reshape(2 * tokens, padded)
        values = rows[:, :width]
        first = (width // 128) * 128
        tail = rows[:, first:].astype(jnp.float32)
        lanes = lax.broadcasted_iota(jnp.int32, tail.shape, 1) + first - width
        chosen = (lanes == me) | (lanes == me + experts)
        weight = jnp.sum(jnp.where(chosen, tail, 0.0), axis=1, keepdims=True)
        gate = dot_t(values, gate_w[...])
        up = dot_t(values, up_w[...])
        activated = (gate / (1.0 + jnp.exp(-gate)) * up).astype(jnp.bfloat16)
        result = jnp.dot(activated, down_w[...], preferred_element_type=jnp.float32)
        result = (result * weight).astype(jnp.bfloat16)
        part_buf[block] = result.reshape(2, tokens, width)
        mate_copy(block).start()

    def compute(step, mine):
        def one(way, carry):
            at_line, exists = place(step, way)
            block = chip(at_line, jnp.where(mine, side, 1 - side))

            @pl.when(exists)
            def _():
                for chunk in range(CHUNKS):
                    rows_arrived(block, chunk, other)
                expert(block)

            return carry

        lax.fori_loop(0, 2, one, 0)

    def side_sum(step):
        def one(way, carry):
            at_line, exists = place(step, way)
            block = chip(at_line, 1 - side)

            @pl.when(exists)
            def _():
                mate_copy(block).wait_recv()

                def part(chunk, inner):
                    span = rows_of(chunk)
                    total = part_buf[block, core, span].astype(jnp.float32)
                    total = total + mate_buf[block, span].astype(jnp.float32)
                    part_buf[block, core, span] = total.astype(jnp.bfloat16)

                    @pl.when(jnp.logical_not(crosses_first(at_line, chunk)))
                    def _():
                        side_copy(at_line, chunk).start()

                    return inner

                lax.fori_loop(0, CHUNKS, part, 0)

            return carry

        lax.fori_loop(0, 2, one, 0)

    early = max(depth - 2, 0)

    def gather_step(index, carry):
        step = index // CHUNKS
        chunk = index % CHUNKS

        @pl.when(index == CHUNKS)
        def _():
            for load in loads:
                load.wait()

        @pl.when(index == (depth + 1) * CHUNKS + 1)
        def _():
            side_sum(early)

        compute(jnp.where(chunk == 0, step - 1, step - 2), chunk == 0)

        def relay_line(way, inner):
            at_line, exists = place(step, way)
            block = chip(at_line, side)

            @pl.when(exists)
            def _():
                @pl.when(step > 0)
                def _():
                    rows_arrived(block, chunk, core)

                @pl.when(has_up & (at_line <= line))
                def _():
                    rows_copy(block, chunk, 2, up_id).start()

                @pl.when(has_down & (at_line >= line))
                def _():
                    rows_copy(block, chunk, 3, down_id).start()

                @pl.when((step == 0) | jnp.logical_not(crosses_first(at_line, chunk)))
                def _():
                    rows_copy(block, chunk, 1, side_id).start()

                rows_copy(block, chunk, 0, mate_id).start()

            return inner

        def relay_side(way, inner):
            at_line, exists = place(step - 1, way)
            block = chip(at_line, 1 - side)

            @pl.when(exists)
            def _():
                rows_arrived(block, chunk, core)
                crossed = crosses_first(at_line, chunk)

                @pl.when(crossed & has_up & (at_line <= line))
                def _():
                    rows_copy(block, chunk, 2, up_id).start()

                @pl.when(crossed & has_down & (at_line >= line))
                def _():
                    rows_copy(block, chunk, 3, down_id).start()

                rows_copy(block, chunk, 0, mate_id).start()

            return inner

        lax.fori_loop(0, 2, relay_line, 0)
        lax.fori_loop(0, 2, relay_side, 0)
        return carry

    lax.fori_loop(0, (depth + 2) * CHUNKS, gather_step, 0)

    def side_step(index, carry):
        step = depth - 1 - index

        @pl.when(step != early)
        def _():
            side_sum(step)

        return carry

    lax.fori_loop(0, depth, side_step, 0)

    def mate_total(at_line, chunk):
        block = chip(at_line, side)
        span = rows_of(chunk)
        total = part_buf[block, core, span].astype(jnp.float32)
        return total + mate_buf[block, span].astype(jnp.float32)

    def line_total(at_line, chunk):
        side_copy(at_line, chunk).wait_recv()
        return mate_total(at_line, chunk) + side_buf[at_line, rows_of(chunk)].astype(jnp.float32)

    def line_step(index, carry):
        step = depth - 1 - index // (2 * CHUNKS)
        chunk = CHUNKS - 1 - index // 2 % CHUNKS
        at_line, exists = place(step, index % 2)
        block = chip(at_line, side)
        span = rows_of(chunk)

        @pl.when(exists)
        def _():
            upward = at_line > line
            way = jnp.where(upward, 0, 1)
            feeds = jnp.where(upward, has_down, has_up)

            crossed = crosses_first(at_line, chunk)

            @pl.when(chunk == CHUNKS - 1)
            def _():
                mate_copy(block).wait_recv()

            @pl.when(crossed & feeds)
            def _():
                far_add(at_line, way)

            @pl.when(crossed & upward)
            def _():
                far_copy(at_line, 0, up_id).start()

            @pl.when(crossed & jnp.logical_not(upward))
            def _():
                far_copy(at_line, 1, down_id).start()

            @pl.when(crossed)
            def _():
                part_buf[block, core, span] = mate_total(at_line, chunk).astype(jnp.bfloat16)

            @pl.when(jnp.logical_not(crossed))
            def _():
                part_buf[block, core, span] = line_total(at_line, chunk).astype(jnp.bfloat16)

            @pl.when(feeds)
            def _():
                line_copy(at_line, chunk, way, up_id).wait_recv()
                total = part_buf[block, core, span].astype(jnp.float32)
                total = total + line_buf[way, at_line, span].astype(jnp.float32)
                part_buf[block, core, span] = total.astype(jnp.bfloat16)

            @pl.when(upward)
            def _():
                line_copy(at_line, chunk, 0, up_id).start()

            @pl.when(jnp.logical_not(upward))
            def _():
                line_copy(at_line, chunk, 1, down_id).start()

        return carry

    lax.fori_loop(0, 2 * CHUNKS * (depth - 1), line_step, 0)

    mate_copy(me).wait_recv()

    for at_end, way in ((line == 0, 1), (line == depth - 1, 0)):

        @pl.when(at_end)
        def _():
            far_add(line, way)
            side_copy(line, CHUNKS - 1).start()

    def finish(chunk, carry):
        span = rows_of(chunk)
        for exists, way in ((has_down, 0), (has_up, 1)):

            @pl.when(exists)
            def _():
                line_copy(line, chunk, way, up_id).wait_recv()
                hidden_ref[span, :] = hidden_ref[span, :] + line_buf[way, line, span].astype(
                    jnp.float32
                )

        total = hidden_ref[span, :] + line_total(line, chunk)
        out_ref[span, :] = total.astype(out_ref.dtype)
        return carry

    lax.fori_loop(0, CHUNKS, finish, 0)

    def drain(at_line, carry):
        block = chip(at_line, side)
        across = chip(at_line, 1 - side)
        mate_copy(block).wait_send()
        mate_copy(across).wait_send()
        for chunk in range(CHUNKS):
            rows_copy(block, chunk, 0, mate_id).wait_send()
            crossed = crosses_first(at_line, chunk)

            @pl.when(jnp.logical_not(crossed) | (at_line == line))
            def _():
                rows_copy(block, chunk, 1, side_id).wait_send()
                side_copy(at_line, chunk).wait_send()

            rows_copy(across, chunk, 0, mate_id).wait_send()

            @pl.when(crossed & has_up & (at_line <= line))
            def _():
                rows_copy(across, chunk, 2, up_id).wait_send()

            @pl.when(crossed & has_down & (at_line >= line))
            def _():
                rows_copy(across, chunk, 3, down_id).wait_send()

            @pl.when(crossed & (at_line != line))
            def _():
                far_copy(at_line, jnp.where(at_line == 0, 1, 0), up_id).wait_send()

            @pl.when(has_up & (at_line <= line))
            def _():
                rows_copy(block, chunk, 2, up_id).wait_send()

            @pl.when(has_down & (at_line >= line))
            def _():
                rows_copy(block, chunk, 3, down_id).wait_send()

            @pl.when(at_line != line)
            def _():
                line_copy(at_line, chunk, 0, up_id).wait_send()

        return carry

    lax.fori_loop(0, depth, drain, 0)


def routed_experts(rows, hidden_state, w_gate, w_up, w_down):
    experts = lax.axis_size("att")
    depth = experts // INNER
    tokens, padded = rows.shape
    width = hidden_state.shape[1]
    inner = w_gate.shape[2]
    bf16 = jnp.bfloat16
    dma = pltpu.SemaphoreType.DMA
    vmem = pl.BlockSpec(memory_space=pltpu.VMEM)
    hbm = pl.BlockSpec(memory_space=pl.ANY)

    def body(*refs):
        x_ref, hidden_in, *rest = refs
        hidden = rest[-1]
        hidden[...] = hidden_in[...]
        moe_kernel(depth, x_ref, hidden, *rest[:-1])

    return pl.pallas_call(
        body,
        out_shape=jax.ShapeDtypeStruct((tokens, width), bf16),
        in_specs=[vmem, vmem, hbm, hbm, hbm],
        out_specs=vmem,
        scratch_shapes=[
            pltpu.VMEM((experts, 2, tokens, padded), bf16),
            pltpu.VMEM((experts, 2, tokens, width), bf16),
            pltpu.VMEM((experts, tokens, width), bf16),
            pltpu.VMEM((depth, tokens, width), bf16),
            pltpu.VMEM((2, depth, tokens, width), bf16),
            pltpu.VMEM((inner, width), bf16),
            pltpu.VMEM((inner, width), bf16),
            pltpu.VMEM((inner, width), bf16),
            dma((3,)),
            dma,
            dma((experts, CHUNKS, 4)),
            dma((experts, CHUNKS, 2)),
            dma((experts,)),
            dma((experts,)),
            dma((depth, CHUNKS)),
            dma((depth, CHUNKS)),
            dma((depth, CHUNKS)),
            dma((2, depth, CHUNKS)),
            pltpu.VMEM((2, tokens // CHUNKS, width), bf16),
            dma((2,)),
            dma((2,)),
            pltpu.VMEM((tokens, width), jnp.float32),
        ],
        compiler_params=pltpu.CompilerParams(
            collective_id=0, has_side_effects=True, vmem_limit_bytes=62 * 1024 * 1024
        ),
    )(rows, hidden_state, jnp.swapaxes(w_gate, 1, 2), jnp.swapaxes(w_up, 1, 2), w_down)


def attend_block(query, new_key, new_value, keys, values, lengths):
    rows = query.shape[0]
    heads = query.shape[1] // HEAD
    lane_heads = new_key.shape[1] // HEAD
    group = heads // lane_heads
    cache_len = keys.shape[1]
    pair = 2 * HEAD
    inverse_root = 1.0 / math.sqrt(HEAD)
    lanes = lax.broadcasted_iota(jnp.int32, (rows, pair), 1)
    low = lanes < HEAD
    pieces = []
    for head in range(heads):
        tile = query[:, (head // 2) * pair : (head // 2 + 1) * pair]
        lane_head = head // group
        if head % 2 != lane_head:
            tile = pltpu.roll(tile, HEAD, 1)
        pieces.append(jnp.where(low if lane_head == 0 else jnp.logical_not(low), tile, 0.0))
    stacked = jnp.concatenate(pieces, axis=0)
    tall_key = jnp.concatenate([new_key] * heads, axis=0)
    tall_value = jnp.concatenate([new_value] * heads, axis=0)
    fresh = jnp.sum(stacked * tall_key, axis=1, keepdims=True) * inverse_root
    scores = dot_t(stacked.astype(jnp.bfloat16), keys.reshape(rows * cache_len, pair)) * inverse_root
    position = lax.broadcasted_iota(jnp.int32, scores.shape, 1)
    row = lax.broadcasted_iota(jnp.int32, (scores.shape[0], 1), 0)
    request = row % rows
    start = request * cache_len
    tall_length = jnp.zeros_like(row)
    for at in range(rows):
        tall_length = jnp.where(request == at, lengths[at], tall_length)
    live = (position >= start) & (position < start + tall_length)
    scores = jnp.where(live, scores, -1e30)
    highest = jnp.maximum(jnp.max(scores, axis=1, keepdims=True), fresh)
    cached_exp = jnp.exp(scores - highest)
    fresh_exp = jnp.exp(fresh - highest)
    scale = 1.0 / (jnp.sum(cached_exp, axis=1, keepdims=True) + fresh_exp)
    probs = (cached_exp * scale).astype(jnp.bfloat16)
    fresh_probs = (fresh_exp * scale).astype(jnp.bfloat16).astype(jnp.float32)
    output = jnp.dot(
        probs, values.reshape(rows * cache_len, pair), preferred_element_type=jnp.float32
    )
    output = output + fresh_probs * tall_value
    tiles = []
    for at in range(heads // 2):
        first = output[2 * at * rows : (2 * at + 1) * rows]
        second = output[(2 * at + 1) * rows : (2 * at + 2) * rows]
        if (2 * at) // group == 0:
            second = pltpu.roll(second, HEAD, 1)
        else:
            first = pltpu.roll(first, HEAD, 1)
        tiles.append(jnp.where(low, first, second))
    return jnp.concatenate(tiles, axis=1)


STEP = 16
HALF = 8
SPAN = 768


def attention_kernel(
    experts,
    query_ref,
    new_key_ref,
    new_value_ref,
    lengths_ref,
    residual_ref,
    gain_ref,
    router_ref,
    routes_ref,
    keys_hbm,
    values_hbm,
    proj_hbm,
    rows_ref,
    hidden_ref,
    keys_buf,
    values_buf,
    proj_w,
    attended,
    sent,
    landed,
    wide_router,
    keys_sem,
    values_sem,
    proj_sem,
    send_sem,
    recv_sem,
):
    core = lax.axis_index("exp")
    other = 1 - core
    mate = {"exp": other}
    barrier = pltpu.get_barrier_semaphore()
    pl.semaphore_signal(barrier, inc=1, device_id=mate, device_id_type=pl.DeviceIdType.MESH)
    requests = query_ref.shape[0]
    tokens, width = residual_ref.shape
    steps = requests // STEP

    def cache_load(step):
        span = pl.ds(step * STEP, STEP)
        return (
            pltpu.make_async_copy(keys_hbm.at[span], keys_buf.at[span], keys_sem.at[step]),
            pltpu.make_async_copy(values_hbm.at[span], values_buf.at[span], values_sem.at[step]),
        )

    proj_load = pltpu.make_async_copy(proj_hbm, proj_w, proj_sem)
    for step in range(steps):
        for load in cache_load(step):
            load.start()
    proj_load.start()

    first = (width // 128) * 128
    base = width - first
    wide_router[...] = jnp.zeros_like(wide_router)
    wide_router[base : base + experts, :] = router_ref[...]
    wide_router[base + experts : base + 2 * experts, :] = router_ref[...]

    def attend_step(step, carry):
        span = pl.ds(pl.multiple_of(step * STEP, STEP), STEP)
        for load in cache_load(step):
            load.wait()
        query = query_ref[span, :].astype(jnp.float32)
        new_key = new_key_ref[span, :].astype(jnp.float32)
        new_value = new_value_ref[span, :].astype(jnp.float32)
        keys = keys_buf[span]
        values = values_buf[span]
        parts = []
        for half in range(STEP // HALF):
            cut = slice(half * HALF, (half + 1) * HALF)
            lengths = [lengths_ref[step * STEP + half * HALF + at] for at in range(HALF)]
            parts.append(
                attend_block(
                    query[cut], new_key[cut], new_value[cut], keys[cut], values[cut], lengths
                )
            )
        attended[span, :] = jnp.concatenate(parts, axis=0).astype(jnp.bfloat16)
        return carry

    lax.fori_loop(0, steps, attend_step, 0)

    proj_load.wait()
    pl.semaphore_wait(barrier, 1)
    theirs = attended[pl.ds(pl.multiple_of(other * tokens, tokens), tokens), :]
    mine = attended[pl.ds(pl.multiple_of(core * tokens, tokens), tokens), :]
    both = jnp.concatenate([theirs, mine], axis=0)
    copies = []
    for at, begin in enumerate(range(0, width, SPAN)):
        end = min(begin + SPAN, width)
        product = dot_t(both, proj_w[begin:end, :])
        sent[at, :, : end - begin] = product[:tokens]
        copy = pltpu.make_async_remote_copy(
            src_ref=sent.at[at],
            dst_ref=landed.at[at],
            send_sem=send_sem.at[at],
            recv_sem=recv_sem.at[at],
            device_id=mate,
            device_id_type=pl.DeviceIdType.MESH,
        )
        copy.start()
        copies.append(copy)
        hidden_ref[:, begin:end] = (
            residual_ref[:, begin:end].astype(jnp.float32) + product[tokens:]
        )
    squares = jnp.zeros((tokens, 1), jnp.float32)
    for at, begin in enumerate(range(0, width, SPAN)):
        end = min(begin + SPAN, width)
        copies[at].wait_recv()
        total = hidden_ref[:, begin:end] + landed[at, :, : end - begin]
        hidden_ref[:, begin:end] = total
        squares = squares + jnp.sum(total * total, axis=1, keepdims=True)
    scale = lax.rsqrt(squares / width + 1e-05)
    normed = (hidden_ref[...] * scale * gain_ref[...].reshape(1, width)).astype(jnp.bfloat16)
    pieces = []
    rest = wide_router[...]
    for _ in range(3):
        piece = rest.astype(jnp.bfloat16)
        rest = rest - piece.astype(jnp.float32)
        pieces.append(piece)
    logits = dot_t(normed, pieces[0]) + (dot_t(normed, pieces[1]) + dot_t(normed, pieces[2]))
    lane = lax.broadcasted_iota(jnp.int32, logits.shape, 1) - base
    coarse_lane = (lane >= 0) & (lane < experts)
    fine_lane = (lane >= experts) & (lane < 2 * experts)
    column = lax.broadcasted_iota(jnp.int32, (logits.shape[1], 1), 0) - base
    column = jnp.where(column >= experts, column - experts, column)
    hits = jnp.zeros((logits.shape[1], tokens), jnp.float32)
    for at in range(routes_ref.shape[0]):
        hits = jnp.where(routes_ref[at : at + 1, :] == column, 1.0, hits)
    named = hits.T > 0.5
    squashed = jnp.where(named, 1.0 / (1.0 + jnp.exp(-logits)), 0.0)
    totals = jnp.sum(jnp.where(coarse_lane, squashed, 0.0), axis=1, keepdims=True)
    weight = squashed / totals
    coarse = weight.astype(jnp.bfloat16).astype(jnp.float32)
    tail = jnp.where(coarse_lane, coarse, jnp.where(fine_lane, weight - coarse, 0.0))
    rows_ref[:, :width] = normed
    rows_ref[:, width:] = tail[:, base:].astype(jnp.bfloat16)
    for copy in copies:
        copy.wait_send()


def attention_layer(
    query, new_key, new_value, cache_keys, cache_values, lengths, out_proj, residual, gain, router, routes
):
    experts = lax.axis_size("att")
    requests = query.shape[0]
    tokens, width = residual.shape
    padded = pl.cdiv(width + 2 * experts, 128) * 128
    spans = pl.cdiv(width, SPAN)
    vmem = pl.BlockSpec(memory_space=pltpu.VMEM)
    hbm = pl.BlockSpec(memory_space=pl.ANY)
    bf16 = jnp.bfloat16
    dma = pltpu.SemaphoreType.DMA

    def body(*refs):
        attention_kernel(experts, *refs)

    return pl.pallas_call(
        body,
        out_shape=(
            jax.ShapeDtypeStruct((tokens, padded), bf16),
            jax.ShapeDtypeStruct((tokens, width), jnp.float32),
        ),
        in_specs=[vmem] * 3 + [pl.BlockSpec(memory_space=pltpu.SMEM)] + [vmem] * 4 + [hbm] * 3,
        out_specs=(vmem, vmem),
        scratch_shapes=[
            pltpu.VMEM(cache_keys.shape, bf16),
            pltpu.VMEM(cache_values.shape, bf16),
            pltpu.VMEM((width, out_proj.shape[0]), bf16),
            pltpu.VMEM(query.shape, bf16),
            pltpu.VMEM((spans, tokens, SPAN), jnp.float32),
            pltpu.VMEM((spans, tokens, SPAN), jnp.float32),
            pltpu.VMEM((128, width), jnp.float32),
            dma((requests // STEP,)),
            dma((requests // STEP,)),
            dma,
            dma((spans,)),
            dma((spans,)),
        ],
        compiler_params=pltpu.CompilerParams(
            collective_id=1, has_side_effects=True, vmem_limit_bytes=62 * 1024 * 1024
        ),
    )(
        query,
        new_key,
        new_value,
        lengths,
        residual,
        gain,
        router.T,
        routes.T,
        cache_keys,
        cache_values,
        out_proj.T,
    )


def per_device(
    query,
    new_key,
    new_value,
    cache_keys,
    cache_values,
    lengths,
    out_proj,
    residual,
    norm_gain,
    router,
    routes,
    w_gate,
    w_up,
    w_down,
):
    rows, hidden_state = attention_layer(
        query,
        new_key,
        new_value,
        cache_keys,
        cache_values,
        lengths,
        out_proj,
        residual,
        norm_gain,
        router,
        routes,
    )
    return routed_experts(rows, hidden_state, w_gate, w_up, w_down)


def solution(mesh):
    in_specs = (
        P(("groups", "att"), "exp"),
        P(("groups", "att"), "exp"),
        P(("groups", "att"), "exp"),
        P(("groups", "att"), None, "exp"),
        P(("groups", "att"), None, "exp"),
        P(("groups", "att")),
        P("exp", None),
        P(("groups", "att", "exp"), None),
        P(),
        P(),
        P(("groups", "att", "exp"), None),
        P("att", None, "exp"),
        P("att", None, "exp"),
        P("att", "exp", None),
    )
    out_specs = P(("groups", "att", "exp"), None)
    return jax.shard_map(
        per_device, mesh=mesh, in_specs=in_specs, out_specs=out_specs, check_vma=False
    )
```
